128 devices in a mesh: dp: 32 (over y, z, core), sp: 4 (over x).
Axes of the slice: x: 4, y: 4, z: 4, core: 2. Of those that a mesh axis runs over, the one named last changes fastest.
Arguments:
- queries: bfloat16 [32, 512, 4096], P('dp', 'sp'), may hold values from -30 to 30
- rotated_span_keys: bfloat16 [32, 512, 512], P('dp', 'sp'), may hold values from -6 to 6
- span_value_heads: bfloat16 [32, 512, 512], P('dp', 'sp'), may hold values from -6 to 6
- cache_keys: bfloat16 [32, 4, 8192, 128], P('dp', 'sp'), may hold values from -6 to 6
- cached_prefix_values: bfloat16 [32, 4, 8192, 128], P('dp', 'sp'), may hold values from -6 to 6
- out_weight: bfloat16 [4096, 8192], P('sp', 'dp'), may hold values from -0.09375 to 0.09375
- prefix_lengths: int32 [32], replicated, may hold values from 2 to 8192, as said below
- valid_lengths: int32 [32], replicated, may hold values from 256 to 512, as said below
Outputs:
- output: bfloat16 [32, 512, 8192], P('dp', 'sp')
The draws below stay inside these ranges and needn't reach their ends.
Inputs may be any that keep to these rules, and one draw needn't show every extreme that they name: Trajectory b's live cache slots are 0 to prefix_lengths[b] - 1; some trajectory has exactly 8192. Span positions from valid_lengths[b] on are padding; some trajectory has exactly 512.
All inputs are finite; a program needn't handle non-finite values.
Results may differ from the reference program's by a relative error of at most 0.013.
Values may be sent and summed in bfloat16 or wider, within the bound.
No kernel may reach another device: no remote copies, remote signals or barrier semaphores. Data moves between devices by JAX's collectives and lax.ppermute only.
A program may use at most 128 MiB of HBM per device.

```python
import math
import jax
import jax.numpy as jnp
from jax import lax

D = 8192
QUERY_HEADS = 32
KEY_VALUE_HEADS = 4
HEAD_WIDTH = 128
SPAN_POSITIONS = 512
PREFIX_SLOTS = 8192
TRAJECTORY_COUNT = 32


def draw_queries(key, part):
    starting_offset = jnp.clip(jax.random.normal(jax.random.fold_in(key, 1), (TRAJECTORY_COUNT, SPAN_POSITIONS, QUERY_HEADS, HEAD_WIDTH), jnp.float32), -6.0, 6.0)
    return starting_offset.reshape(TRAJECTORY_COUNT, SPAN_POSITIONS, QUERY_HEADS * HEAD_WIDTH).astype(jnp.bfloat16)


def draw_cache_keys(key, part):
    starting_offset = jnp.clip(jax.random.normal(jax.random.fold_in(key, 2), (TRAJECTORY_COUNT, KEY_VALUE_HEADS, PREFIX_SLOTS, HEAD_WIDTH), jnp.float32), -6.0, 6.0)
    return starting_offset.astype(jnp.bfloat16)


def draw_prefix_lengths(key, part):
    folded = jax.random.fold_in(key, 21)
    first_key, second_key, third_key = jax.random.split(folded, 3)
    first_draw = jax.random.randint(first_key, (TRAJECTORY_COUNT,), 1, PREFIX_SLOTS + 1, dtype=jnp.int32)
    second_draw = jax.random.randint(second_key, (TRAJECTORY_COUNT,), 1, PREFIX_SLOTS + 1, dtype=jnp.int32)
    lengths = jnp.maximum(first_draw * second_draw // PREFIX_SLOTS, 2)
    chosen = jax.random.randint(third_key, (), 0, TRAJECTORY_COUNT, dtype=jnp.int32)
    return lengths.at[chosen].set(PREFIX_SLOTS).astype(jnp.int32)


def draw_valid_lengths(key, part):
    folded = jax.random.fold_in(key, 31)
    first_key, second_key = jax.random.split(folded, 2)
    lengths = jax.random.randint(first_key, (TRAJECTORY_COUNT,), SPAN_POSITIONS // 2, SPAN_POSITIONS + 1, dtype=jnp.int32)
    chosen = jax.random.randint(second_key, (), 0, TRAJECTORY_COUNT, dtype=jnp.int32)
    return lengths.at[chosen].set(SPAN_POSITIONS).astype(jnp.int32)


def levels(stream_key, extent, shards, least, largest):
    level, own = 1.0, jax.random.fold_in(stream_key, 6)
    for position, blocks in shards:
        heights = jnp.exp(jax.random.uniform(jax.random.fold_in(own, position), (blocks,), jnp.float32, least / len(shards), largest / len(shards)))
        level = level * jnp.repeat(heights, extent[position] // blocks).reshape([-1 if axis == position else 1 for axis in range(len(extent))])
    return level


def normal_values(rng, dims, spread, limit, cuts=(), kind=jnp.bfloat16):
    values = spread * jax.random.normal(rng, dims, jnp.float32)
    if cuts:
        values = values * levels(rng, dims, cuts, -0.22, 0.18)
    return jnp.clip(values, -limit, limit).astype(kind)


def setup_inputs(seed: int = 0) -> dict:
    key_list = jax.random.split(jax.random.key(seed), 9)
    return {
        "queries": draw_queries(jax.random.fold_in(key_list[8], 71), 0),
        "rotated_span_keys": normal_values(key_list[1], (TRAJECTORY_COUNT, SPAN_POSITIONS, KEY_VALUE_HEADS * HEAD_WIDTH), 1.0, 6.0, ((0, 32), (1, 4))),
        "span_value_heads": normal_values(key_list[2], (TRAJECTORY_COUNT, SPAN_POSITIONS, KEY_VALUE_HEADS * HEAD_WIDTH), 1.0, 6.0, ((0, 32), (1, 4))),
        "cache_keys": draw_cache_keys(jax.random.fold_in(key_list[8], 71), 0),
        "cached_prefix_values": normal_values(key_list[4], (TRAJECTORY_COUNT, KEY_VALUE_HEADS, PREFIX_SLOTS, HEAD_WIDTH), 1.0, 6.0, ((0, 32), (1, 4))),
        "out_weight": normal_values(key_list[5], (QUERY_HEADS * HEAD_WIDTH, D), (QUERY_HEADS * HEAD_WIDTH) ** -0.5, 0.09375, ((0, 4), (1, 32))),
        "prefix_lengths": draw_prefix_lengths(jax.random.fold_in(key_list[8], 71), 0),
        "valid_lengths": draw_valid_lengths(jax.random.fold_in(key_list[8], 71), 0),
    }


NEGATIVE = -1e+30

def trajectory_output(inputs, out_weight):
    query_tile_block, current_span_key, current_span_value, prefix_key, prefix_value, prefix_length, valid_length = inputs
    group_width = QUERY_HEADS // KEY_VALUE_HEADS
    query_head_rows = query_tile_block.astype(jnp.float32).reshape(SPAN_POSITIONS, KEY_VALUE_HEADS, group_width, HEAD_WIDTH).transpose(1, 2, 0, 3)
    fresh_keys = current_span_key.astype(jnp.float32).reshape(SPAN_POSITIONS, KEY_VALUE_HEADS, HEAD_WIDTH).transpose(1, 0, 2)
    fresh_values = current_span_value.astype(jnp.float32).reshape(SPAN_POSITIONS, KEY_VALUE_HEADS, HEAD_WIDTH).transpose(1, 0, 2)
    all_keys = jnp.concatenate([prefix_key.astype(jnp.float32), fresh_keys], axis=1)
    all_values = jnp.concatenate([prefix_value.astype(jnp.float32), fresh_values], axis=1)
    scores = jnp.einsum('grtd,gkd->grtk', query_head_rows, all_keys) * (1.0 / math.sqrt(HEAD_WIDTH))
    key_position = jnp.arange(PREFIX_SLOTS + SPAN_POSITIONS, dtype=jnp.int32)
    query_position = jnp.arange(SPAN_POSITIONS, dtype=jnp.int32)
    usable = jnp.where(key_position[None, :] < PREFIX_SLOTS, key_position[None, :] < prefix_length, key_position[None, :] - PREFIX_SLOTS <= query_position[:, None])
    scores = jnp.where(usable, scores, NEGATIVE)
    highest = lax.optimization_barrier(jnp.max(scores, axis=-1, keepdims=True))
    weights = jnp.exp(scores - highest)
    totals = lax.optimization_barrier(jnp.sum(weights, axis=-1))
    rounded = lax.optimization_barrier(weights.astype(jnp.bfloat16)).astype(jnp.float32)
    mixed = jnp.einsum('grtk,gkd->grtd', rounded, all_values) / totals[..., None]
    attended = mixed.transpose(2, 0, 1, 3).reshape(SPAN_POSITIONS, QUERY_HEADS * HEAD_WIDTH).astype(jnp.bfloat16)
    projected = jnp.dot(attended, out_weight, preferred_element_type=jnp.float32).astype(jnp.bfloat16)
    keep_rows = jnp.arange(SPAN_POSITIONS, dtype=jnp.int32) < valid_length
    return jnp.where(keep_rows[:, None], projected, jnp.zeros_like(projected))

def reference(queries, rotated_span_keys, span_value_heads, cache_keys, cached_prefix_values, out_weight, prefix_lengths, valid_lengths):

    def single(inputs):
        return trajectory_output(inputs, out_weight)
    return lax.map(single, (queries, rotated_span_keys, span_value_heads, cache_keys, cached_prefix_values, prefix_lengths, valid_lengths))
```

```python
import functools
import math

import jax
import jax.numpy as jnp
from jax import lax
from jax.experimental import pallas as pl
from jax.experimental.pallas import tpu as pltpu
from jax.sharding import PartitionSpec as P

NEGATIVE = -1e30
VMEM_LIMIT = 48 << 20
KEY_BLOCK = 4096
ROW_CHUNK = 128


def attention_kernel(
    scalars, q_ref, s0_ref, s1_ref, s2_ref, s3_ref, k_ref, v_ref, o_ref, rows, span, high, total, *, factor
):
    step = pl.program_id(0)
    head_dim = k_ref.shape[1]
    positions = q_ref.shape[0]
    heads = q_ref.shape[1] // head_dim
    row_count = heads * positions
    key_block = k_ref.shape[0]
    chunk = min(ROW_CHUNK, row_count)
    length = scalars[0]
    first_position = scalars[2]
    live = first_position < scalars[1]

    def update(keys, values, usable):
        augmented = jnp.concatenate([values, jnp.ones_like(values)], axis=1)

        def score(start):
            return lax.dot_general(
                rows[start : start + chunk, :],
                keys,
                (((1,), (1,)), ((), ())),
                preferred_element_type=jnp.float32,
            )

        following = score(0)
        for start in range(0, row_count, chunk):
            scores = following
            if start + chunk < row_count:
                following = score(start + chunk)
            if usable is not None:
                scores = jnp.where(usable(start, scores.shape), scores, NEGATIVE)
            block = pl.ds(start, chunk)
            before = high[block, :]
            after = jnp.maximum(before, jnp.max(scores, axis=1, keepdims=True))
            high[block, :] = after
            rescale = jnp.exp2((before - after) * factor)
            weights = jnp.exp2((scores - after[:, :1]) * factor).astype(jnp.bfloat16)
            total[block, :] = total[block, :] * jnp.concatenate([rescale, rescale], axis=1) + jnp.dot(
                weights, augmented, preferred_element_type=jnp.float32
            )

    @pl.when(jnp.logical_and(step == 0, live))
    def _():
        for head in range(heads):
            rows[head * positions : (head + 1) * positions, :] = q_ref[:, head * head_dim : (head + 1) * head_dim]
        high[...] = jnp.full_like(high, NEGATIVE)
        total[...] = jnp.zeros_like(total)
        width = s0_ref.shape[0]
        for index, source in enumerate((s0_ref, s1_ref, s2_ref, s3_ref)):
            span[index * width : (index + 1) * width, :] = source[...]

        def causal(start, shape):
            query = first_position + (start + lax.broadcasted_iota(jnp.int32, shape, 0)) % positions
            column = lax.broadcasted_iota(jnp.int32, shape, 1)
            key = scalars[3] + column
            for index in range(1, 4):
                key = jnp.where(column >= index * width, scalars[3 + index] + column - index * width, key)
            return key <= query

        update(span[:, :head_dim], span[:, head_dim:], causal)

    before_block = (step - 1) * key_block

    @pl.when(jnp.logical_and(live, jnp.logical_and(step > 0, step * key_block <= length)))
    def _():
        update(k_ref[...], v_ref[...], None)

    @pl.when(
        jnp.logical_and(
            live,
            jnp.logical_and(step > 0, jnp.logical_and(before_block < length, step * key_block > length)),
        )
    )
    def _():
        def stored(start, shape):
            return before_block + lax.broadcasted_iota(jnp.int32, shape, 1) < length

        update(k_ref[...], v_ref[...], stored)

    @pl.when(step == pl.num_programs(0) - 1)
    def _():
        @pl.when(live)
        def _():
            for head in range(heads):
                block = slice(head * positions, (head + 1) * positions)
                o_ref[:, head * head_dim : (head + 1) * head_dim] = (
                    total[block, :head_dim] / total[block, head_dim:]
                ).astype(o_ref.dtype)

        @pl.when(jnp.logical_not(live))
        def _():
            o_ref[...] = jnp.zeros_like(o_ref)


def attend(scalars, query, fresh, keys, values):
    positions, features = query.shape
    stored, head_dim = keys.shape
    key_block = math.gcd(KEY_BLOCK, stored)
    blocks = stored // key_block
    row_count = positions * features // head_dim
    width = fresh[0].shape[0]

    def cached(step, scalars):
        last = lax.div(scalars[0] - 1, key_block)
        return (jnp.clip(step - 1, 0, last), 0)

    def whole(step, scalars):
        return (0, 0)

    flops = 4 * row_count * (stored + 4 * width) * head_dim * 2
    return pl.pallas_call(
        functools.partial(attention_kernel, factor=math.log2(math.e) / math.sqrt(head_dim)),
        grid_spec=pltpu.PrefetchScalarGridSpec(
            num_scalar_prefetch=1,
            grid=(blocks + 1,),
            in_specs=[pl.BlockSpec((positions, features), whole)]
            + [pl.BlockSpec((width, 2 * head_dim), whole)] * 4
            + [pl.BlockSpec((key_block, head_dim), cached)] * 2,
            out_specs=pl.BlockSpec((positions, features), whole),
            scratch_shapes=[
                pltpu.VMEM((row_count, head_dim), jnp.bfloat16),
                pltpu.VMEM((4 * width, 2 * head_dim), jnp.bfloat16),
                pltpu.VMEM((row_count, head_dim), jnp.float32),
                pltpu.VMEM((row_count, 2 * head_dim), jnp.float32),
            ],
        ),
        out_shape=jax.ShapeDtypeStruct((positions, features), jnp.bfloat16),
        compiler_params=pltpu.CompilerParams(vmem_limit_bytes=VMEM_LIMIT),
        cost_estimate=pl.CostEstimate(
            flops=flops, bytes_accessed=4 * stored * head_dim, transcendentals=row_count * stored
        ),
        name="attend",
    )(scalars, query, *fresh, keys, values)


def project_kernel(*refs, column_blocks, added, outs):
    mine_ref, other_ref, w_ref = refs[:3]
    add_refs = refs[3 : 3 + len(added)]
    out_refs = refs[3 + len(added) : 3 + len(added) + outs]
    step = pl.program_id(0)
    width = w_ref.shape[2]
    positions = mine_ref.shape[0]
    for index in range(column_blocks):
        columns = slice(index * width, (index + 1) * width)
        for half, source in enumerate((mine_ref, other_ref)):
            block = slice(half * positions, (half + 1) * positions)
            product = jnp.dot(source[...], w_ref[index], preferred_element_type=jnp.float32)
            for (low, high), add_ref in zip(added, add_refs):
                inside = jnp.logical_and(step >= low, step < high)
                product = product + jnp.where(inside, add_ref[block, columns].astype(jnp.float32), 0.0)
            if outs == 1:
                out_refs[0][block, columns] = product.astype(jnp.bfloat16)
            else:
                steps = pl.num_programs(0)
                for part in range(outs):

                    @pl.when(step * outs // steps == part)
                    def _(product=product, part=part):
                        out_refs[part][block, columns] = product.astype(jnp.bfloat16)


def project(mine, other, weight, added=(), outs=1):
    positions, depth = mine.shape
    blocks, _, width = weight.shape
    column_blocks = 2
    steps = blocks // column_blocks
    tile = column_blocks * width
    rows = 2 * positions

    def within(low, high):
        return lambda step: (0, jnp.clip(step - low, 0, high - low - 1))

    share = steps // outs
    out = pl.pallas_call(
        functools.partial(
            project_kernel, column_blocks=column_blocks, added=[(low, high) for _, low, high in added], outs=outs
        ),
        grid=(steps,),
        in_specs=[
            pl.BlockSpec((positions, depth), lambda step: (0, 0)),
            pl.BlockSpec((positions, depth), lambda step: (0, 0)),
            pl.BlockSpec((column_blocks, depth, width), lambda step: (step, 0, 0)),
        ]
        + [pl.BlockSpec((rows, tile), within(low, high)) for _, low, high in added],
        out_specs=[pl.BlockSpec((rows, tile), within(part * share, (part + 1) * share)) for part in range(outs)],
        out_shape=[jax.ShapeDtypeStruct((rows, share * tile), jnp.bfloat16) for _ in range(outs)],
        compiler_params=pltpu.CompilerParams(vmem_limit_bytes=VMEM_LIMIT),
        cost_estimate=pl.CostEstimate(
            flops=2 * rows * depth * blocks * width, bytes_accessed=2 * depth * blocks * width, transcendentals=0
        ),
        name="project",
    )(mine, other, weight, *[array for array, _, _ in added])
    return out


def combine_kernel(scalars, even_ref, odd_ref, o_ref, *, width):
    positions = even_ref.shape[0]
    keep = scalars[1] + lax.broadcasted_iota(jnp.int32, (positions, width), 0) < scalars[0]
    zero = jnp.zeros((positions, width), jnp.bfloat16)
    own, arrived = even_ref, odd_ref
    flip = scalars[2] == 1
    for index in range(own.shape[1] // width):
        columns = slice(index * width, (index + 1) * width)
        first = jnp.where(keep, own[:, columns], zero)
        second = jnp.where(keep, arrived[:, columns], zero)
        left = jnp.where(flip, second, first)
        right = jnp.where(flip, first, second)
        o_ref[0, :, 2 * index * width : (2 * index + 1) * width] = left
        o_ref[0, :, (2 * index + 1) * width : (2 * index + 2) * width] = right


def combine(scalars, own, arrived, width):
    positions, columns = own.shape
    steps = 4
    tile = columns // steps
    return pl.pallas_call(
        functools.partial(combine_kernel, width=width),
        grid_spec=pltpu.PrefetchScalarGridSpec(
            num_scalar_prefetch=1,
            grid=(steps,),
            in_specs=[pl.BlockSpec((positions, tile), lambda step, scalars: (0, step))] * 2,
            out_specs=pl.BlockSpec((1, positions, 2 * tile), lambda step, scalars: (0, 0, step)),
        ),
        out_shape=jax.ShapeDtypeStruct((1, positions, 2 * columns), jnp.bfloat16),
        compiler_params=pltpu.CompilerParams(vmem_limit_bytes=VMEM_LIMIT),
        name="combine",
    )(scalars, own, arrived)


def local(
    queries,
    rotated_span_keys,
    span_value_heads,
    cache_keys,
    cached_prefix_values,
    out_weight,
    prefix_lengths,
    valid_lengths,
):
    parts = lax.axis_size("sp")
    rows = lax.axis_size("dp")
    me = lax.axis_index("sp")
    row = lax.axis_index("dp")
    positions = queries.shape[1]
    head_dim = cache_keys.shape[3]
    features = queries.shape[2] // parts

    same_core = [list(range(core, rows, 2)) for core in range(2)]
    weight = lax.all_gather(out_weight, "dp", axis=0, tiled=False, axis_index_groups=same_core)

    def shift(array, distance):
        return lax.ppermute(array, "sp", [(i, (i + distance) % parts) for i in range(parts)])

    def swap(array):
        return lax.ppermute(array, "dp", [(i, i ^ 1) for i in range(rows)])

    def part_of(array, owner, size):
        return lax.dynamic_slice_in_dim(array, owner * size, size, 1)

    position = [(me + distance) % parts for distance in range(parts)]
    fresh_parts, query_parts = [], []
    for distance in range(parts):
        owner = position[distance]
        pair = jnp.concatenate(
            [
                part_of(rotated_span_keys[0], owner, head_dim),
                part_of(span_value_heads[0], owner, head_dim),
            ],
            axis=1,
        )
        fresh_parts.append(pair if distance == 0 else shift(pair, distance))
    for distance in range(parts):
        part = part_of(queries[0], position[distance], features)
        query_parts.append(part if distance == 0 else shift(part, distance))
    fresh = [fresh_parts[(parts - distance) % parts] for distance in range(parts)]
    query = [query_parts[(parts - distance) % parts] for distance in range(parts)]

    own_prefix = lax.dynamic_index_in_dim(prefix_lengths, row, 0, keepdims=False)
    own_valid = lax.dynamic_index_in_dim(valid_lengths, row, 0, keepdims=False)
    starts = [place * positions for place in position]

    def attended(distance, begin, size):
        scalars = jnp.stack([own_prefix, own_valid, starts[distance] + begin] + starts).astype(jnp.int32)
        block = lax.slice_in_dim(query[distance], begin, begin + size, axis=0)
        mine = attend(scalars, block, fresh, cache_keys[0, 0], cached_prefix_values[0, 0])
        return mine, swap(mine)

    half = positions // 2
    steps = weight.shape[0] // 2

    far = attended(2, 0, positions)
    send_right, send_left = project(*far, weight, outs=2)
    from_left, from_right = shift(send_right, 1), shift(send_left, -1)

    def rows_of(array, begin):
        return jnp.concatenate(
            [array[begin : begin + half], array[positions + begin : positions + begin + half]], axis=0
        )

    arrived = []
    for begin in (0, half):
        right = attended(1, begin, half)
        (to_right,) = project(*right, weight, added=[(rows_of(from_left, begin), 0, steps // 2)])
        right_in = shift(to_right, 1)
        left = attended(3, begin, half)
        (to_left,) = project(*left, weight, added=[(rows_of(from_right, begin), steps // 2, steps)])
        left_in = shift(to_left, -1)
        arrived.append((right_in, left_in))

    results = []
    own = attended(0, 0, positions)
    (total,) = project(*own, weight)
    scalars = jnp.stack([own_valid, starts[0], row % 2]).astype(jnp.int32)
    for index, begin in enumerate((0, half)):
        first, second = arrived[index]
        summed = (
            rows_of(total, begin).astype(jnp.float32) + first.astype(jnp.float32) + second.astype(jnp.float32)
        ).astype(jnp.bfloat16)
        results.append(summed)
    mine = jnp.concatenate([results[0][:half], results[1][:half]], axis=0)
    theirs = jnp.concatenate([results[0][half:], results[1][half:]], axis=0)
    return combine(scalars, mine, swap(theirs), weight.shape[2])


def solution(mesh):
    in_specs = (
        P("dp", "sp", None),
        P("dp", "sp", None),
        P("dp", "sp", None),
        P("dp", "sp", None, None),
        P("dp", "sp", None, None),
        P("sp", "dp"),
        P(),
        P(),
    )
    out_specs = P("dp", "sp", None)
    return jax.shard_map(local, mesh=mesh, in_specs=in_specs, out_specs=out_specs, check_vma=False)
```

```python
import functools
import math

import jax
import jax.numpy as jnp
from jax import lax
from jax.experimental import pallas as pl
from jax.experimental.pallas import tpu as pltpu
from jax.sharding import PartitionSpec as P

NEGATIVE = -1e30
VMEM_LIMIT = 48 << 20
KEY_BLOCK = 4096
ROW_CHUNK = 128


def attention_kernel(
    prefix_lengths,
    valid_lengths,
    q_ref,
    s0_ref,
    s1_ref,
    s2_ref,
    s3_ref,
    k_ref,
    v_ref,
    o_ref,
    rows,
    span,
    high,
    total,
    *,
    distance,
    factor,
):
    step = pl.program_id(0)
    head_dim = k_ref.shape[1]
    positions = q_ref.shape[0]
    heads = o_ref.shape[1] // head_dim
    row_count = heads * positions
    key_block = k_ref.shape[0]
    chunk = min(ROW_CHUNK, row_count)
    parts = lax.axis_size("sp")
    me = lax.axis_index("sp")
    row = lax.axis_index("dp")
    length = prefix_lengths[row]

    def start_of(offset):
        return lax.rem(me + offset, parts) * positions

    first_position = start_of(distance)
    live = first_position < valid_lengths[row]

    def update(keys, values, usable):
        augmented = jnp.concatenate([values, jnp.ones_like(values)], axis=1)

        def score(start):
            return lax.dot_general(
                rows[pl.ds(start, chunk), :],
                keys,
                (((1,), (1,)), ((), ())),
                preferred_element_type=jnp.float32,
            )

        def fold(start, scores):
            if usable is not None:
                scores = jnp.where(usable(scores.shape), scores, NEGATIVE)
            block = pl.ds(start, chunk)
            before = high[block, :]
            after = jnp.maximum(before, jnp.max(scores, axis=1, keepdims=True))
            high[block, :] = after
            rescale = jnp.exp2((before - after) * factor)
            weights = jnp.exp2((scores - after[:, :1]) * factor).astype(jnp.bfloat16)
            total[block, :] = total[block, :] * jnp.concatenate([rescale, rescale], axis=1) + jnp.dot(
                weights, augmented, preferred_element_type=jnp.float32
            )

        if usable is not None:

            @pl.loop(0, row_count // chunk)
            def _(index):
                start = pl.multiple_of(index * chunk, chunk)
                fold(start, score(start))

            return
        following = score(0)
        for start in range(0, row_count, chunk):
            scores = following
            if start + chunk < row_count:
                following = score(start + chunk)
            fold(start, scores)

    @pl.when(jnp.logical_and(step == 0, live))
    def _():
        for head in range(heads):
            rows[head * positions : (head + 1) * positions, :] = q_ref[:, head * head_dim : (head + 1) * head_dim]
        high[...] = jnp.full_like(high, NEGATIVE)
        total[...] = jnp.zeros_like(total)
        for index, source in enumerate((s0_ref, s1_ref, s2_ref, s3_ref)):
            span[index * positions : (index + 1) * positions, :] = source[:, source.shape[1] - 2 * head_dim :]

        def causal(shape):
            query = first_position + lax.rem(lax.broadcasted_iota(jnp.int32, shape, 0), positions)
            column = lax.broadcasted_iota(jnp.int32, shape, 1)
            key = start_of(0) + column
            for index in range(1, parts):
                key = jnp.where(column >= index * positions, start_of(index) + column - index * positions, key)
            return key <= query

        update(span[:, :head_dim], span[:, head_dim:], causal)

    before_block = (step - 1) * key_block

    @pl.when(jnp.logical_and(live, jnp.logical_and(step > 0, step * key_block <= length)))
    def _():
        update(k_ref[...], v_ref[...], None)

    @pl.when(
        jnp.logical_and(
            live,
            jnp.logical_and(step > 0, jnp.logical_and(before_block < length, step * key_block > length)),
        )
    )
    def _():
        def stored(shape):
            return before_block + lax.broadcasted_iota(jnp.int32, shape, 1) < length

        update(k_ref[...], v_ref[...], stored)

    @pl.when(step == pl.num_programs(0) - 1)
    def _():
        @pl.when(live)
        def _():
            for head in range(heads):
                block = slice(head * positions, (head + 1) * positions)
                o_ref[:, head * head_dim : (head + 1) * head_dim] = (
                    total[block, :head_dim] / total[block, head_dim:]
                ).astype(o_ref.dtype)

        @pl.when(jnp.logical_not(live))
        def _():
            o_ref[...] = jnp.zeros_like(o_ref)


def attend(prefix_lengths, valid_lengths, blocks, distance, keys, values):
    positions, features = blocks[0].shape
    stored, head_dim = keys.shape
    features -= 2 * head_dim
    key_block = math.gcd(KEY_BLOCK, stored)
    count = stored // key_block
    row_count = positions * features // head_dim

    def cached(step, prefix_lengths, valid_lengths):
        last = lax.div(prefix_lengths[lax.axis_index("dp")] - 1, key_block)
        return (jnp.clip(step - 1, 0, last), 0)

    def whole(step, *_):
        return (0, 0)

    flops = 8 * row_count * (stored + 4 * positions) * head_dim
    return pl.pallas_call(
        functools.partial(attention_kernel, distance=distance, factor=math.log2(math.e) / math.sqrt(head_dim)),
        grid_spec=pltpu.PrefetchScalarGridSpec(
            num_scalar_prefetch=2,
            grid=(count + 1,),
            in_specs=[pl.BlockSpec((positions, features + 2 * head_dim), whole)] * 5
            + [pl.BlockSpec((key_block, head_dim), cached)] * 2,
            out_specs=pl.BlockSpec((positions, features), whole),
            scratch_shapes=[
                pltpu.VMEM((row_count, head_dim), jnp.bfloat16),
                pltpu.VMEM((4 * positions, 2 * head_dim), jnp.bfloat16),
                pltpu.VMEM((row_count, head_dim), jnp.float32),
                pltpu.VMEM((row_count, 2 * head_dim), jnp.float32),
            ],
        ),
        out_shape=jax.ShapeDtypeStruct((positions, features), jnp.bfloat16),
        compiler_params=pltpu.CompilerParams(vmem_limit_bytes=VMEM_LIMIT),
        cost_estimate=pl.CostEstimate(
            flops=flops, bytes_accessed=4 * stored * head_dim, transcendentals=row_count * stored
        ),
        name="attend",
    )(prefix_lengths, valid_lengths, blocks[distance], *blocks, keys, values)


def project_kernel(mine_ref, other_ref, w_ref, *refs):
    add_ref = refs[0] if len(refs) == 3 else None
    o_ref, both = refs[-2:]
    positions = mine_ref.shape[0]

    @pl.when(pl.program_id(0) == 0)
    def _():
        both[:positions, :] = mine_ref[...]
        both[positions:, :] = other_ref[...]

    width = w_ref.shape[2]
    for index in range(w_ref.shape[0]):
        columns = slice(index * width, (index + 1) * width)
        product = jnp.dot(both[...], w_ref[index], preferred_element_type=jnp.float32)
        if add_ref is not None:
            product = product + add_ref[:, columns].astype(jnp.float32)
        o_ref[:, columns] = product.astype(o_ref.dtype)


def project(pair, weight, first, count, add=None):
    positions, depth = pair[0].shape
    width = weight.shape[2]
    group = math.gcd(count, max(1, 512 // width))
    steps = count // group
    rows = 2 * positions
    tile = group * width

    def column(step):
        return (0, step)

    return pl.pallas_call(
        project_kernel,
        grid=(steps,),
        in_specs=[pl.BlockSpec((positions, depth), lambda step: (0, 0))] * 2
        + [pl.BlockSpec((group, depth, width), lambda step: (step + first // group, 0, 0))]
        + [pl.BlockSpec((rows, tile), column)] * (add is not None),
        out_specs=pl.BlockSpec((rows, tile), column),
        scratch_shapes=[pltpu.VMEM((rows, depth), jnp.bfloat16)],
        out_shape=jax.ShapeDtypeStruct((rows, count * width), jnp.bfloat16),
        compiler_params=pltpu.CompilerParams(vmem_limit_bytes=VMEM_LIMIT),
        cost_estimate=pl.CostEstimate(
            flops=2 * rows * depth * count * width, bytes_accessed=2 * depth * count * width, transcendentals=0
        ),
        name="project",
    )(*pair, weight, *([] if add is None else [add]))


def combine_kernel(valid_lengths, own_ref, arrived_ref, o_ref, *, width):
    positions = own_ref.shape[0]
    start = lax.axis_index("sp") * positions
    row = lax.axis_index("dp")
    keep = start + lax.broadcasted_iota(jnp.int32, (positions, width), 0) < valid_lengths[row]
    zero = jnp.zeros((positions, width), jnp.bfloat16)
    flip = lax.rem(row, 2) == 1
    for index in range(own_ref.shape[1] // width):
        columns = slice(index * width, (index + 1) * width)
        first = jnp.where(keep, own_ref[:, columns], zero)
        second = jnp.where(keep, arrived_ref[:, columns], zero)
        o_ref[0, :, 2 * index * width : (2 * index + 1) * width] = jnp.where(flip, second, first)
        o_ref[0, :, (2 * index + 1) * width : (2 * index + 2) * width] = jnp.where(flip, first, second)


def combine(valid_lengths, own, arrived, width):
    positions, columns = own.shape
    steps = 4
    tile = columns // steps
    return pl.pallas_call(
        functools.partial(combine_kernel, width=width),
        grid_spec=pltpu.PrefetchScalarGridSpec(
            num_scalar_prefetch=1,
            grid=(steps,),
            in_specs=[pl.BlockSpec((positions, tile), lambda step, _: (0, step))] * 2,
            out_specs=pl.BlockSpec((1, positions, 2 * tile), lambda step, _: (0, 0, step)),
        ),
        out_shape=jax.ShapeDtypeStruct((1, positions, 2 * columns), jnp.bfloat16),
        compiler_params=pltpu.CompilerParams(vmem_limit_bytes=VMEM_LIMIT),
        name="combine",
    )(valid_lengths, own, arrived)


def local(
    queries,
    rotated_span_keys,
    span_value_heads,
    cache_keys,
    cached_prefix_values,
    out_weight,
    prefix_lengths,
    valid_lengths,
):
    parts = lax.axis_size("sp")
    rows = lax.axis_size("dp")
    me = lax.axis_index("sp")
    positions = queries.shape[1]
    head_dim = cache_keys.shape[3]
    features = queries.shape[2] // parts

    same_core = [list(range(core, rows, 2)) for core in range(2)]
    weight = lax.all_gather(out_weight, "dp", axis=0, tiled=False, axis_index_groups=same_core)

    def shift(array, distance):
        return lax.ppermute(array, "sp", [(i, (i + distance) % parts) for i in range(parts)])

    def swap(array):
        return lax.ppermute(array, "dp", [(i, i ^ 1) for i in range(rows)])

    def part_of(array, owner, size):
        return lax.dynamic_slice_in_dim(array, owner * size, size, 1)

    def bundle(distance):
        owner = lax.rem(me + distance, parts)
        return jnp.concatenate(
            [
                part_of(queries[0], owner, features),
                part_of(rotated_span_keys[0], owner, head_dim),
                part_of(span_value_heads[0], owner, head_dim),
            ],
            axis=1,
        )

    blocks = [None] * parts
    for distance in (2, 1, 3, 0):
        block = bundle(distance)
        blocks[(parts - distance) % parts] = shift(block, distance) if distance else block

    def attended(distance):
        mine = attend(prefix_lengths, valid_lengths, blocks, distance, cache_keys[0, 0], cached_prefix_values[0, 0])
        return mine, swap(mine)

    pieces = weight.shape[0]
    half = pieces // 2
    far = attended(2)
    from_left = shift(project(far, weight, 0, half), 1)
    from_right = shift(project(far, weight, half, half), -1)
    right = attended(1)
    right_high = shift(project(right, weight, half, half), 1)
    left = attended(3)
    left_low = shift(project(left, weight, 0, half), -1)
    right_low = shift(project(right, weight, 0, half, from_left), 1)
    left_high = shift(project(left, weight, half, half, from_right), -1)
    own = attended(0)
    own_low = project(own, weight, 0, half)
    own_high = project(own, weight, half, half)

    def summed(*terms):
        return sum(term.astype(jnp.float32) for term in terms).astype(jnp.bfloat16)

    low = summed(own_low, right_low, left_low)
    high = summed(own_high, right_high, left_high)
    mine = jnp.concatenate([low[:positions], high[:positions]], axis=1)
    theirs = jnp.concatenate([low[positions:], high[positions:]], axis=1)
    return combine(valid_lengths, mine, swap(theirs), weight.shape[2])


def solution(mesh):
    in_specs = (
        P("dp", "sp", None),
        P("dp", "sp", None),
        P("dp", "sp", None),
        P("dp", "sp", None, None),
        P("dp", "sp", None, None),
        P("sp", "dp"),
        P(),
        P(),
    )
    out_specs = P("dp", "sp", None)
    return jax.shard_map(local, mesh=mesh, in_specs=in_specs, out_specs=out_specs, check_vma=False)
```

```python
import functools
import math

import jax
import jax.numpy as jnp
from jax import lax
from jax.experimental import pallas as pl
from jax.experimental.pallas import tpu as pltpu
from jax.sharding import PartitionSpec as P

NEGATIVE = -1e30
VMEM_LIMIT = 48 << 20
KEY_BLOCK = 4096
KEY_PIECE = 1024
ROW_CHUNK = 128


def attention_kernel(
    prefix_lengths,
    valid_lengths,
    q_ref,
    s0_ref,
    s1_ref,
    s2_ref,
    s3_ref,
    k_ref,
    v_ref,
    o_ref,
    rows,
    span,
    high,
    total,
    *,
    distance,
    factor,
):
    step = pl.program_id(0)
    head_dim = k_ref.shape[1]
    positions = q_ref.shape[0]
    heads = o_ref.shape[1] // head_dim
    row_count = heads * positions
    key_block = k_ref.shape[0]
    chunk = min(ROW_CHUNK, row_count)
    parts = lax.axis_size("sp")
    me = lax.axis_index("sp")
    row = lax.axis_index("dp")
    length = prefix_lengths[row]

    def start_of(offset):
        return lax.rem(me + offset, parts) * positions

    first_position = start_of(distance)
    live = first_position < valid_lengths[row]

    def update(keys, values, usable):
        augmented = jnp.concatenate([values, jnp.ones_like(values)], axis=1)

        def score(start):
            return lax.dot_general(
                rows[pl.ds(start, chunk), :],
                keys,
                (((1,), (1,)), ((), ())),
                preferred_element_type=jnp.float32,
            )

        def fold(start, scores):
            if usable is not None:
                scores = jnp.where(usable(scores.shape), scores, NEGATIVE)
            block = pl.ds(start, chunk)
            before = high[block, :]
            after = jnp.maximum(before, jnp.max(scores, axis=1, keepdims=True))
            high[block, :] = after
            rescale = jnp.exp2((before - after) * factor)
            weights = jnp.exp2((scores - after[:, :1]) * factor).astype(jnp.bfloat16)
            total[block, :] = total[block, :] * jnp.concatenate([rescale, rescale], axis=1) + jnp.dot(
                weights, augmented, preferred_element_type=jnp.float32
            )

        following = score(0)
        for start in range(0, row_count, chunk):
            scores = following
            if start + chunk < row_count:
                following = score(start + chunk)
            fold(start, scores)

    @pl.when(jnp.logical_and(step == 0, live))
    def _():
        for head in range(heads):
            rows[head * positions : (head + 1) * positions, :] = q_ref[:, head * head_dim : (head + 1) * head_dim]
        high[...] = jnp.full_like(high, NEGATIVE)
        total[...] = jnp.zeros_like(total)
        for index, source in enumerate((s0_ref, s1_ref, s2_ref, s3_ref)):
            span[index * positions : (index + 1) * positions, :] = source[...]

        def causal(shape):
            query = first_position + lax.rem(lax.broadcasted_iota(jnp.int32, shape, 0), positions)
            column = lax.broadcasted_iota(jnp.int32, shape, 1)
            key = start_of(0) + column
            for index in range(1, parts):
                key = jnp.where(column >= index * positions, start_of(index) + column - index * positions, key)
            return key <= query

        update(span[:, :head_dim], span[:, head_dim:], causal)

    before_block = (step - 1) * key_block

    @pl.when(jnp.logical_and(live, jnp.logical_and(step > 0, step * key_block <= length)))
    def _():
        update(k_ref[...], v_ref[...], None)

    @pl.when(
        jnp.logical_and(
            live,
            jnp.logical_and(step > 0, jnp.logical_and(before_block < length, step * key_block > length)),
        )
    )
    def _():
        piece = math.gcd(KEY_PIECE, key_block)

        @pl.loop(0, lax.div(length - before_block + piece - 1, piece))
        def _(index):
            begin = pl.multiple_of(index * piece, piece)

            def stored(shape):
                return before_block + begin + lax.broadcasted_iota(jnp.int32, shape, 1) < length

            update(k_ref[pl.ds(begin, piece), :], v_ref[pl.ds(begin, piece), :], stored)

    @pl.when(step == pl.num_programs(0) - 1)
    def _():
        @pl.when(live)
        def _():
            for head in range(heads):
                block = slice(head * positions, (head + 1) * positions)
                o_ref[:, head * head_dim : (head + 1) * head_dim] = (
                    total[block, :head_dim] / total[block, head_dim:]
                ).astype(o_ref.dtype)

        @pl.when(jnp.logical_not(live))
        def _():
            o_ref[...] = jnp.zeros_like(o_ref)


def attend(prefix_lengths, valid_lengths, query, fresh, distance, keys, values):
    positions, features = query.shape
    stored, head_dim = keys.shape
    key_block = math.gcd(KEY_BLOCK, stored)
    count = stored // key_block
    row_count = positions * features // head_dim

    def cached(step, prefix_lengths, valid_lengths):
        last = lax.div(prefix_lengths[lax.axis_index("dp")] - 1, key_block)
        return (jnp.clip(step - 1, 0, last), 0)

    def whole(step, *_):
        return (0, 0)

    flops = 8 * row_count * (stored + 4 * positions) * head_dim
    return pl.pallas_call(
        functools.partial(attention_kernel, distance=distance, factor=math.log2(math.e) / math.sqrt(head_dim)),
        grid_spec=pltpu.PrefetchScalarGridSpec(
            num_scalar_prefetch=2,
            grid=(count + 1,),
            in_specs=[pl.BlockSpec((positions, features), whole)]
            + [pl.BlockSpec((positions, 2 * head_dim), whole)] * 4
            + [pl.BlockSpec((key_block, head_dim), cached)] * 2,
            out_specs=pl.BlockSpec((positions, features), whole),
            scratch_shapes=[
                pltpu.VMEM((row_count, head_dim), jnp.bfloat16),
                pltpu.VMEM((4 * positions, 2 * head_dim), jnp.bfloat16),
                pltpu.VMEM((row_count, head_dim), jnp.float32),
                pltpu.VMEM((row_count, 2 * head_dim), jnp.float32),
            ],
        ),
        out_shape=jax.ShapeDtypeStruct((positions, features), jnp.bfloat16),
        compiler_params=pltpu.CompilerParams(vmem_limit_bytes=VMEM_LIMIT),
        cost_estimate=pl.CostEstimate(
            flops=flops, bytes_accessed=4 * stored * head_dim, transcendentals=row_count * stored
        ),
        name="attend",
    )(prefix_lengths, valid_lengths, query, *fresh, keys, values)


def project_kernel(*refs, starts):
    count = len(starts)
    mine_ref, other_ref = refs[:2]
    w_refs = refs[2 : 2 + count]
    o_ref, both, held, arrivals = refs[-4:]
    add_ref = refs[2 + count] if len(refs) == count + 7 else None
    pieces = held.shape[1]
    copies = []
    for index, start in enumerate(starts):
        copy = pltpu.make_async_copy(w_refs[index].at[start : start + pieces], held.at[index], arrivals.at[index])
        copy.start()
        copies.append(copy)
    positions = mine_ref.shape[0]
    both[:positions, :] = mine_ref[...]
    both[positions:, :] = other_ref[...]
    width = held.shape[3]
    for index, copy in enumerate(copies):
        copy.wait()
        for piece in range(0, pieces, 2):
            begin = (index * pieces + piece) * width
            columns = slice(begin, begin + 2 * width)
            tile = jnp.concatenate([held[index, piece], held[index, piece + 1]], axis=1)
            product = jnp.dot(both[...], tile, preferred_element_type=jnp.float32)
            if add_ref is not None:
                product = product + add_ref[:, columns].astype(jnp.float32)
            o_ref[:, columns] = product.astype(o_ref.dtype)


def project(pair, weights, add=None):
    positions, depth = pair[0].shape
    pieces = 4
    arrays, starts = [], []
    for weight in weights:
        for start in range(0, weight.shape[0], pieces):
            arrays.append(weight)
            starts.append(start)
    width = weights[0].shape[2]
    rows = 2 * positions
    columns = len(starts) * pieces * width
    whole = pl.BlockSpec(memory_space=pltpu.VMEM)
    operands = [*pair, *arrays] + ([] if add is None else [add])
    return pl.pallas_call(
        functools.partial(project_kernel, starts=starts),
        in_specs=[whole] * 2 + [pl.BlockSpec(memory_space=pl.ANY)] * len(arrays) + [whole] * (add is not None),
        out_specs=whole,
        scratch_shapes=[
            pltpu.VMEM((rows, depth), jnp.bfloat16),
            pltpu.VMEM((len(starts), pieces, depth, width), jnp.bfloat16),
            pltpu.SemaphoreType.DMA((len(starts),)),
        ],
        out_shape=jax.ShapeDtypeStruct((rows, columns), jnp.bfloat16),
        compiler_params=pltpu.CompilerParams(vmem_limit_bytes=VMEM_LIMIT),
        cost_estimate=pl.CostEstimate(
            flops=2 * rows * depth * columns, bytes_accessed=2 * depth * columns, transcendentals=0
        ),
        name="project",
    )(*operands)


def place_of(row, side):
    chip = lax.div(row, 2)
    return lax.div(chip, side), lax.rem(chip, side)


def combine_kernel(valid_lengths, *refs, width, side):
    o_ref = refs[-1]
    positions = o_ref.shape[1]
    start = lax.axis_index("sp") * positions
    row = lax.axis_index("dp")
    core = lax.rem(row, 2)
    y, z = place_of(row, side)
    keep = start + lax.broadcasted_iota(jnp.int32, (positions, width), 0) < valid_lengths[row]
    for part in range(2):
        own, first, second, arrived = refs[4 * part : 4 * part + 4]
        for index in range(side * side):
            if part == 0:
                piece = lax.rem(y + index % side, side) * side + lax.rem(z + index // side, side)
            else:
                piece = index
            columns = slice(index * width, (index + 1) * width)
            total = (
                own[:, columns].astype(jnp.float32)
                + first[:, columns].astype(jnp.float32)
                + second[:, columns].astype(jnp.float32)
            )
            for source, value in ((core, total.astype(o_ref.dtype)), (1 - core, arrived[:, columns])):
                column = pl.multiple_of((2 * piece + source) * 2 * width + part * width, width)
                o_ref[0, :, pl.ds(column, width)] = jnp.where(keep, value, jnp.zeros_like(value))


def combine(valid_lengths, parts, positions, width, side):
    columns = parts[0].shape[1]
    spec = pl.BlockSpec((positions, columns), lambda step, _: (0, 0))
    return pl.pallas_call(
        functools.partial(combine_kernel, width=width, side=side),
        grid_spec=pltpu.PrefetchScalarGridSpec(
            num_scalar_prefetch=1,
            grid=(1,),
            in_specs=[spec] * len(parts),
            out_specs=pl.BlockSpec((1, positions, 4 * columns), lambda step, _: (0, 0, 0)),
        ),
        out_shape=jax.ShapeDtypeStruct((1, positions, 4 * columns), jnp.bfloat16),
        compiler_params=pltpu.CompilerParams(vmem_limit_bytes=VMEM_LIMIT),
        name="combine",
    )(valid_lengths, *parts)


def local(
    queries,
    rotated_span_keys,
    span_value_heads,
    cache_keys,
    cached_prefix_values,
    out_weight,
    prefix_lengths,
    valid_lengths,
):
    parts = lax.axis_size("sp")
    rows = lax.axis_size("dp")
    me = lax.axis_index("sp")
    positions = queries.shape[1]
    head_dim = cache_keys.shape[3]
    features = queries.shape[2] // parts

    side = math.isqrt(rows // 2)
    width = out_weight.shape[1] // 2

    def shift(array, distance):
        return lax.ppermute(array, "sp", [(i, (i + distance) % parts) for i in range(parts)])

    def swap(array):
        return lax.ppermute(array, "dp", [(i, i ^ 1) for i in range(rows)])

    def across(array, dy, dz):
        pairs = []
        for i in range(rows):
            y, z, core = i // (2 * side), (i // 2) % side, i % 2
            pairs.append((i, (((y + dy) % side) * side + (z + dz) % side) * 2 + core))
        return lax.ppermute(array, "dp", pairs)

    def after(value, *others):
        return lax.optimization_barrier((value, *others))[0]

    def part_of(array, owner, size):
        return lax.dynamic_slice_in_dim(array, owner * size, size, 1)

    fresh, query = [None] * parts, [None] * parts
    for distance in (2, 1, 3, 0):
        owner = lax.rem(me + distance, parts)
        pair = jnp.concatenate(
            [part_of(rotated_span_keys[0], owner, head_dim), part_of(span_value_heads[0], owner, head_dim)], axis=1
        )
        fresh[(parts - distance) % parts] = shift(pair, distance) if distance else pair
    for distance in (2, 1, 3, 0):
        part = part_of(queries[0], lax.rem(me + distance, parts), features)
        query[(parts - distance) % parts] = shift(part, distance) if distance else part

    same_core = [list(range(core, rows, 2)) for core in range(2)]
    late = lax.all_gather(out_weight[:, width:], "dp", axis=0, tiled=False, axis_index_groups=same_core)
    piece = out_weight[:, :width]
    middle = piece.shape[0] // 2
    before, behind = across(piece, 1, 0), across(piece, -1, 0)
    ahead_top, ahead_bottom = across(before[:middle], 1, 0), across(behind[middle:], -1, 0)

    def attended(distance, *waits):
        mine = attend(
            prefix_lengths,
            valid_lengths,
            after(query[distance], *waits),
            fresh,
            distance,
            cache_keys[0, 0],
            cached_prefix_values[0, 0],
        )
        return mine, swap(mine)

    own = attended(0, before, behind)
    line = jnp.stack([piece, behind, jnp.concatenate([ahead_top, ahead_bottom], axis=0), before])
    line = after(line, own[0])
    line_before, line_behind = across(line, 0, 1), across(line, 0, -1)
    far = attended(2, line)
    line_before, line_behind = after(line_before, far[0]), after(line_behind, far[0])
    opposite = jnp.concatenate(
        [across(line_before[: side // 2], 0, 1), across(line_behind[side // 2 :], 0, -1)], axis=0
    )
    early = [line, line_behind, opposite, line_before]
    right = attended(1, line_before, line_behind)
    left = attended(3, right[0])
    from_left = shift(project(far, early), 1)
    from_right = shift(project(far, [late]), -1)
    left_early = shift(project(left, early), -1)
    right_late = shift(project(right, [late]), 1)
    right_early = shift(project(right, early, from_left), 1)
    left_late = shift(project(left, [late], from_right), -1)
    own_early = project(own, early)
    own_late = project(own, [late])

    def summed(*terms):
        return sum(term[positions:].astype(jnp.float32) for term in terms).astype(jnp.bfloat16)

    early_terms = (own_early, right_early, left_early)
    late_terms = (own_late, right_late, left_late)
    return combine(
        valid_lengths,
        [*early_terms, swap(summed(*early_terms)), *late_terms, swap(summed(*late_terms))],
        positions,
        width,
        side,
    )


def solution(mesh):
    in_specs = (
        P("dp", "sp", None),
        P("dp", "sp", None),
        P("dp", "sp", None),
        P("dp", "sp", None, None),
        P("dp", "sp", None, None),
        P("sp", "dp"),
        P(),
        P(),
    )
    out_specs = P("dp", "sp", None)
    return jax.shard_map(local, mesh=mesh, in_specs=in_specs, out_specs=out_specs, check_vma=False)
```

```python
import functools
import math

import jax
import jax.numpy as jnp
from jax import lax
from jax.experimental import pallas as pl
from jax.experimental.pallas import tpu as pltpu
from jax.sharding import PartitionSpec as P

NEGATIVE = -1e30
VMEM_LIMIT = 48 << 20
KEY_BLOCK = 4096
KEY_PIECE = 1024
ROW_CHUNK = 128


def attention_kernel(
    prefix_lengths,
    valid_lengths,
    q_ref,
    s0_ref,
    s1_ref,
    s2_ref,
    s3_ref,
    k_ref,
    v_ref,
    o_ref,
    rows,
    span,
    high,
    total,
    *,
    distance,
    factor,
):
    step = pl.program_id(0)
    head_dim = k_ref.shape[1]
    positions = q_ref.shape[0]
    heads = o_ref.shape[1] // head_dim
    row_count = heads * positions
    key_block = k_ref.shape[0]
    chunk = min(ROW_CHUNK, row_count)
    parts = lax.axis_size("sp")
    me = lax.axis_index("sp")
    row = lax.axis_index("dp")
    length = prefix_lengths[row]

    def start_of(offset):
        return lax.rem(me + offset, parts) * positions

    first_position = start_of(distance)
    live = first_position < valid_lengths[row]

    def update(keys, values, usable):
        augmented = jnp.concatenate([values, jnp.ones_like(values)], axis=1)

        def score(start):
            return lax.dot_general(
                rows[pl.ds(start, chunk), :],
                keys,
                (((1,), (1,)), ((), ())),
                preferred_element_type=jnp.float32,
            )

        def fold(start, scores):
            if usable is not None:
                scores = jnp.where(usable(scores.shape), scores, NEGATIVE)
            block = pl.ds(start, chunk)
            before = high[block, :]
            after = jnp.maximum(before, jnp.max(scores, axis=1, keepdims=True))
            high[block, :] = after
            rescale = jnp.exp2((before - after) * factor)
            weights = jnp.exp2((scores - after[:, :1]) * factor).astype(jnp.bfloat16)
            total[block, :] = total[block, :] * jnp.concatenate([rescale, rescale], axis=1) + jnp.dot(
                weights, augmented, preferred_element_type=jnp.float32
            )

        following = score(0)
        for start in range(0, row_count, chunk):
            scores = following
            if start + chunk < row_count:
                following = score(start + chunk)
            fold(start, scores)

    @pl.when(jnp.logical_and(step == 0, live))
    def _():
        for head in range(heads):
            rows[head * positions : (head + 1) * positions, :] = q_ref[:, head * head_dim : (head + 1) * head_dim]
        high[...] = jnp.full_like(high, NEGATIVE)
        total[...] = jnp.zeros_like(total)
        for index, source in enumerate((s0_ref, s1_ref, s2_ref, s3_ref)):
            span[index * positions : (index + 1) * positions, :] = source[:, source.shape[1] - 2 * head_dim :]

        def causal(shape):
            query = first_position + lax.rem(lax.broadcasted_iota(jnp.int32, shape, 0), positions)
            column = lax.broadcasted_iota(jnp.int32, shape, 1)
            key = start_of(0) + column
            for index in range(1, parts):
                key = jnp.where(column >= index * positions, start_of(index) + column - index * positions, key)
            return key <= query

        update(span[:, :head_dim], span[:, head_dim:], causal)

    before_block = (step - 1) * key_block

    @pl.when(jnp.logical_and(live, jnp.logical_and(step > 0, step * key_block <= length)))
    def _():
        update(k_ref[...], v_ref[...], None)

    @pl.when(
        jnp.logical_and(
            live,
            jnp.logical_and(step > 0, jnp.logical_and(before_block < length, step * key_block > length)),
        )
    )
    def _():
        piece = math.gcd(KEY_PIECE, key_block)

        @pl.loop(0, lax.div(length - before_block + piece - 1, piece))
        def _(index):
            begin = pl.multiple_of(index * piece, piece)

            def stored(shape):
                return before_block + begin + lax.broadcasted_iota(jnp.int32, shape, 1) < length

            update(k_ref[pl.ds(begin, piece), :], v_ref[pl.ds(begin, piece), :], stored)

    @pl.when(step == pl.num_programs(0) - 1)
    def _():
        @pl.when(live)
        def _():
            for head in range(heads):
                block = slice(head * positions, (head + 1) * positions)
                o_ref[:, head * head_dim : (head + 1) * head_dim] = (
                    total[block, :head_dim] / total[block, head_dim:]
                ).astype(o_ref.dtype)

        @pl.when(jnp.logical_not(live))
        def _():
            o_ref[...] = jnp.zeros_like(o_ref)


def attend(prefix_lengths, valid_lengths, query, blocks, distance, keys, values):
    positions, features = query.shape
    stored, head_dim = keys.shape
    features -= 2 * head_dim
    key_block = math.gcd(KEY_BLOCK, stored)
    count = stored // key_block
    row_count = positions * features // head_dim

    def cached(step, prefix_lengths, valid_lengths):
        last = lax.div(prefix_lengths[lax.axis_index("dp")] - 1, key_block)
        return (jnp.clip(step - 1, 0, last), 0)

    def whole(step, *_):
        return (0, 0)

    flops = 8 * row_count * (stored + 4 * positions) * head_dim
    return pl.pallas_call(
        functools.partial(attention_kernel, distance=distance, factor=math.log2(math.e) / math.sqrt(head_dim)),
        grid_spec=pltpu.PrefetchScalarGridSpec(
            num_scalar_prefetch=2,
            grid=(count + 1,),
            in_specs=[pl.BlockSpec((positions, features + 2 * head_dim), whole)] * 5
            + [pl.BlockSpec((key_block, head_dim), cached)] * 2,
            out_specs=pl.BlockSpec((positions, features), whole),
            scratch_shapes=[
                pltpu.VMEM((row_count, head_dim), jnp.bfloat16),
                pltpu.VMEM((4 * positions, 2 * head_dim), jnp.bfloat16),
                pltpu.VMEM((row_count, head_dim), jnp.float32),
                pltpu.VMEM((row_count, 2 * head_dim), jnp.float32),
            ],
        ),
        out_shape=jax.ShapeDtypeStruct((positions, features), jnp.bfloat16),
        compiler_params=pltpu.CompilerParams(vmem_limit_bytes=VMEM_LIMIT),
        cost_estimate=pl.CostEstimate(
            flops=flops, bytes_accessed=4 * stored * head_dim, transcendentals=row_count * stored
        ),
        name="attend",
    )(prefix_lengths, valid_lengths, query, *blocks, keys, values)


def project_kernel(*refs, adds, outs):
    count = len(adds)
    mine_ref, other_ref = refs[:2]
    w_refs = refs[2 : 2 + count]
    add_refs = refs[2 + count : -outs - 3]
    o_refs = refs[-outs - 3 : -3]
    both, held, arrivals = refs[-3:]
    copies = []
    for index in range(count):
        copy = pltpu.make_async_copy(w_refs[index], held.at[index], arrivals.at[index])
        copy.start()
        copies.append(copy)
    positions = mine_ref.shape[0]
    both[:positions, :] = mine_ref[...]
    both[positions:, :] = other_ref[...]
    pieces, width = held.shape[1], held.shape[3]
    share = count // outs
    for index, copy in enumerate(copies):
        copy.wait()
        o_ref = o_refs[index // share]
        for piece in range(0, pieces, 2):
            tile = jnp.concatenate([held[index, piece], held[index, piece + 1]], axis=1)
            product = jnp.dot(both[...], tile, preferred_element_type=jnp.float32)
            if adds[index] is not None:
                begin = (adds[index] * pieces + piece) * width
                product = product + add_refs[0][:, begin : begin + 2 * width].astype(jnp.float32)
            begin = (index % share * pieces + piece) * width
            o_ref[:, begin : begin + 2 * width] = product.astype(o_ref.dtype)


def project(pair, weights, add=None, added=0, outs=1):
    positions, depth = pair[0].shape
    pieces, _, width = weights[0].shape
    rows = 2 * positions
    count = len(weights)
    columns = count * pieces * width
    covered = 0 if add is None else add.shape[1] // (pieces * width)
    adds = [index - added if added <= index < added + covered else None for index in range(count)]
    whole = pl.BlockSpec(memory_space=pltpu.VMEM)
    return pl.pallas_call(
        functools.partial(project_kernel, adds=adds, outs=outs),
        in_specs=[whole] * 2 + [pl.BlockSpec(memory_space=pl.ANY)] * count + [whole] * (add is not None),
        out_specs=[whole] * outs,
        scratch_shapes=[
            pltpu.VMEM((rows, depth), jnp.bfloat16),
            pltpu.VMEM((count, pieces, depth, width), jnp.bfloat16),
            pltpu.SemaphoreType.DMA((count,)),
        ],
        out_shape=[jax.ShapeDtypeStruct((rows, columns // outs), jnp.bfloat16)] * outs,
        compiler_params=pltpu.CompilerParams(vmem_limit_bytes=VMEM_LIMIT),
        cost_estimate=pl.CostEstimate(
            flops=2 * rows * depth * columns, bytes_accessed=2 * depth * columns, transcendentals=0
        ),
        name="project",
    )(*pair, *weights, *([] if add is None else [add]))


def place_of(row, side):
    chip = lax.div(row, 2)
    return lax.div(chip, side), lax.rem(chip, side)


def combine_kernel(valid_lengths, *refs, groups, width, side):
    o_ref = refs[-1]
    positions = o_ref.shape[1]
    start = lax.axis_index("sp") * positions
    row = lax.axis_index("dp")
    core = lax.rem(row, 2)
    y, z = place_of(row, side)
    keep = start + lax.broadcasted_iota(jnp.int32, (positions, width), 0) < valid_lengths[row]
    for part, members in enumerate(groups):
        own, first, second, arrived = refs[4 * part : 4 * part + 4]
        for index, (kind, offset) in enumerate(members):
            for step in range(side):
                dy, dz = (step, offset) if kind == 0 else (offset, step)
                piece = lax.rem(y + dy, side) * side + lax.rem(z + dz, side)
                columns = slice((index * side + step) * width, (index * side + step + 1) * width)
                total = (
                    own[:, columns].astype(jnp.float32)
                    + first[:, columns].astype(jnp.float32)
                    + second[:, columns].astype(jnp.float32)
                )
                for source, value in ((core, total.astype(o_ref.dtype)), (1 - core, arrived[:, columns])):
                    column = pl.multiple_of((2 * piece + source) * 2 * width + kind * width, width)
                    o_ref[0, :, pl.ds(column, width)] = jnp.where(keep, value, jnp.zeros_like(value))


def combine(valid_lengths, parts, groups, positions, width, side):
    columns = 4 * width * side * side
    return pl.pallas_call(
        functools.partial(combine_kernel, groups=groups, width=width, side=side),
        grid_spec=pltpu.PrefetchScalarGridSpec(
            num_scalar_prefetch=1,
            grid=(1,),
            in_specs=[pl.BlockSpec((positions, part.shape[1]), lambda step, _: (0, 0)) for part in parts],
            out_specs=pl.BlockSpec((1, positions, columns), lambda step, _: (0, 0, 0)),
        ),
        out_shape=jax.ShapeDtypeStruct((1, positions, columns), jnp.bfloat16),
        compiler_params=pltpu.CompilerParams(vmem_limit_bytes=VMEM_LIMIT),
        name="combine",
    )(valid_lengths, *parts)


def local(
    queries,
    rotated_span_keys,
    span_value_heads,
    cache_keys,
    cached_prefix_values,
    out_weight,
    prefix_lengths,
    valid_lengths,
):
    parts = lax.axis_size("sp")
    rows = lax.axis_size("dp")
    me = lax.axis_index("sp")
    positions = queries.shape[1]
    head_dim = cache_keys.shape[3]
    features = queries.shape[2] // parts

    side = math.isqrt(rows // 2)
    width = out_weight.shape[1] // 2

    def shift(array, distance):
        return lax.ppermute(array, "sp", [(i, (i + distance) % parts) for i in range(parts)])

    def swap(array):
        return lax.ppermute(array, "dp", [(i, i ^ 1) for i in range(rows)])

    def across(array, dy, dz):
        pairs = []
        for i in range(rows):
            y, z, core = i // (2 * side), (i // 2) % side, i % 2
            pairs.append((i, (((y + dy) % side) * side + (z + dz) % side) * 2 + core))
        return lax.ppermute(array, "dp", pairs)

    def after(value, *others):
        return lax.optimization_barrier((value, *others))[0]

    def part_of(array, owner, size):
        return lax.dynamic_slice_in_dim(array, owner * size, size, 1)

    def gather_line(piece, dy, dz):
        return [piece, across(piece, -dy, -dz), across(piece, 2 * dy, 2 * dz), across(piece, dy, dz)]

    pieces = [out_weight[:, :width], out_weight[:, width:]]
    lines = [gather_line(pieces[0], 1, 0), gather_line(pieces[1], 0, 1)]
    blocks = [None] * parts
    for distance in (2, 1, 3, 0):
        owner = lax.rem(me + distance, parts)
        block = jnp.concatenate(
            [
                part_of(queries[0], owner, features),
                part_of(rotated_span_keys[0], owner, head_dim),
                part_of(span_value_heads[0], owner, head_dim),
            ],
            axis=1,
        )
        blocks[(parts - distance) % parts] = shift(block, distance) if distance else block

    def attended(distance, *waits):
        mine = attend(
            prefix_lengths,
            valid_lengths,
            after(blocks[distance], *waits) if waits else blocks[distance],
            blocks,
            distance,
            cache_keys[0, 0],
            cached_prefix_values[0, 0],
        )
        return mine, swap(mine)

    lines = [jnp.stack(line) for line in lines]
    behind = [across(lines[0], 0, 1), across(lines[1], 1, 0)]
    ahead = [across(lines[0], 0, -1), across(lines[1], -1, 0)]
    far = attended(2, *lines)
    right = attended(1, far[0])
    half = side // 2
    behind_part = [after(array[:half], right[0]) for array in behind]
    ahead_part = [after(array[half:], right[0]) for array in ahead]
    opposite = [
        jnp.concatenate([across(behind_part[0], 0, 1), across(ahead_part[0], 0, -1)], axis=0),
        jnp.concatenate([across(behind_part[1], 1, 0), across(ahead_part[1], -1, 0)], axis=0),
    ]
    early = [lines[0], ahead[0], behind[0], lines[1], ahead[1], behind[1]]
    early_groups = [(0, 0), (0, 1), (0, 3), (1, 0), (1, 1), (1, 3)]
    late_groups = [(0, 2), (1, 2)]

    far_right, far_left = project(far, early, outs=2)
    from_left, from_right = shift(far_right, 1), shift(far_left, -1)
    left = attended(3, right[0], far_right, *behind_part, *ahead_part)
    (right_early,) = project(right, early, from_left, 0)
    (left_early,) = project(left, early, from_right, 3)
    far_right, far_left = project(far, opposite, outs=2)
    from_left_late, from_right_late = shift(far_right, 1), shift(far_left, -1)
    own = attended(0, left_early, right_early, far_right)
    right_in, left_in = shift(right_early, 1), shift(left_early, -1)
    (right_late,) = project(right, opposite, from_left_late, 0)
    (left_late,) = project(left, opposite, from_right_late, 1)
    right_late_in, left_late_in = shift(right_late, 1), shift(left_late, -1)
    (own_early,) = project(own, early)
    (own_late,) = project(own, opposite)

    def summed(*terms):
        return sum(term[positions:].astype(jnp.float32) for term in terms).astype(jnp.bfloat16)

    early_terms = (own_early, right_in, left_in)
    late_terms = (own_late, right_late_in, left_late_in)
    return combine(
        valid_lengths,
        [*early_terms, swap(summed(*early_terms)), *late_terms, swap(summed(*late_terms))],
        [early_groups, late_groups],
        positions,
        width,
        side,
    )


def solution(mesh):
    in_specs = (
        P("dp", "sp", None),
        P("dp", "sp", None),
        P("dp", "sp", None),
        P("dp", "sp", None, None),
        P("dp", "sp", None, None),
        P("sp", "dp"),
        P(),
        P(),
    )
    out_specs = P("dp", "sp", None)
    return jax.shard_map(local, mesh=mesh, in_specs=in_specs, out_specs=out_specs, check_vma=False)
```

```python
import functools
import math

import jax
import jax.numpy as jnp
from jax import lax
from jax.experimental import pallas as pl
from jax.experimental.pallas import tpu as pltpu
from jax.sharding import PartitionSpec as P

NEGATIVE = -1e30
VMEM_LIMIT = 48 << 20
KEY_BLOCK = 4096
KEY_PIECE = 1024
ROW_CHUNK = 128


def attention_kernel(
    prefix_lengths,
    valid_lengths,
    q_ref,
    s0_ref,
    s1_ref,
    s2_ref,
    s3_ref,
    k_ref,
    v_ref,
    o_ref,
    rows,
    span,
    high,
    total,
    *,
    distance,
    factor,
):
    step = pl.program_id(0)
    head_dim = k_ref.shape[1]
    positions = q_ref.shape[0]
    heads = o_ref.shape[1] // head_dim
    row_count = heads * positions
    key_block = k_ref.shape[0]
    chunk = min(ROW_CHUNK, row_count)
    parts = lax.axis_size("sp")
    me = lax.axis_index("sp")
    row = lax.axis_index("dp")
    length = prefix_lengths[row]

    def start_of(offset):
        return lax.rem(me + offset, parts) * positions

    first_position = start_of(distance)
    live = first_position < valid_lengths[row]

    def update(keys, values, usable):
        augmented = jnp.concatenate([values, jnp.ones_like(values)], axis=1)

        def score(start):
            return lax.dot_general(
                rows[pl.ds(start, chunk), :],
                keys,
                (((1,), (1,)), ((), ())),
                preferred_element_type=jnp.float32,
            )

        def fold(start, scores):
            if usable is not None:
                scores = jnp.where(usable(scores.shape), scores, NEGATIVE)
            block = pl.ds(start, chunk)
            before = high[block, :]
            after = jnp.maximum(before, jnp.max(scores, axis=1, keepdims=True))
            high[block, :] = after
            rescale = jnp.exp2((before - after) * factor)
            weights = jnp.exp2((scores - after[:, :1]) * factor).astype(jnp.bfloat16)
            total[block, :] = total[block, :] * jnp.concatenate([rescale, rescale], axis=1) + jnp.dot(
                weights, augmented, preferred_element_type=jnp.float32
            )

        following = score(0)
        for start in range(0, row_count, chunk):
            scores = following
            if start + chunk < row_count:
                following = score(start + chunk)
            fold(start, scores)

    @pl.when(jnp.logical_and(step == 0, live))
    def _():
        for head in range(heads):
            rows[head * positions : (head + 1) * positions, :] = q_ref[:, head * head_dim : (head + 1) * head_dim]
        high[...] = jnp.full_like(high, NEGATIVE)
        total[...] = jnp.zeros_like(total)
        for index, source in enumerate((s0_ref, s1_ref, s2_ref, s3_ref)):
            span[index * positions : (index + 1) * positions, :] = source[...]

        def causal(shape):
            query = first_position + lax.rem(lax.broadcasted_iota(jnp.int32, shape, 0), positions)
            column = lax.broadcasted_iota(jnp.int32, shape, 1)
            key = start_of(0) + column
            for index in range(1, parts):
                key = jnp.where(column >= index * positions, start_of(index) + column - index * positions, key)
            return key <= query

        update(span[:, :head_dim], span[:, head_dim:], causal)

    before_block = (step - 1) * key_block

    @pl.when(jnp.logical_and(live, jnp.logical_and(step > 0, step * key_block <= length)))
    def _():
        update(k_ref[...], v_ref[...], None)

    @pl.when(
        jnp.logical_and(
            live,
            jnp.logical_and(step > 0, jnp.logical_and(before_block < length, step * key_block > length)),
        )
    )
    def _():
        piece = math.gcd(KEY_PIECE, key_block)

        @pl.loop(0, lax.div(length - before_block + piece - 1, piece))
        def _(index):
            begin = pl.multiple_of(index * piece, piece)

            def stored(shape):
                return before_block + begin + lax.broadcasted_iota(jnp.int32, shape, 1) < length

            update(k_ref[pl.ds(begin, piece), :], v_ref[pl.ds(begin, piece), :], stored)

    @pl.when(step == pl.num_programs(0) - 1)
    def _():
        @pl.when(live)
        def _():
            for head in range(heads):
                block = slice(head * positions, (head + 1) * positions)
                o_ref[:, head * head_dim : (head + 1) * head_dim] = (
                    total[block, :head_dim] / total[block, head_dim:]
                ).astype(o_ref.dtype)

        @pl.when(jnp.logical_not(live))
        def _():
            o_ref[...] = jnp.zeros_like(o_ref)


def attend(prefix_lengths, valid_lengths, query, fresh, distance, keys, values):
    positions, features = query.shape
    stored, head_dim = keys.shape
    key_block = math.gcd(KEY_BLOCK, stored)
    count = stored // key_block
    row_count = positions * features // head_dim

    def cached(step, prefix_lengths, valid_lengths):
        last = lax.div(prefix_lengths[lax.axis_index("dp")] - 1, key_block)
        return (jnp.clip(step - 1, 0, last), 0)

    def whole(step, *_):
        return (0, 0)

    flops = 8 * row_count * (stored + 4 * positions) * head_dim
    return pl.pallas_call(
        functools.partial(attention_kernel, distance=distance, factor=math.log2(math.e) / math.sqrt(head_dim)),
        grid_spec=pltpu.PrefetchScalarGridSpec(
            num_scalar_prefetch=2,
            grid=(count + 1,),
            in_specs=[pl.BlockSpec((positions, features), whole)]
            + [pl.BlockSpec((positions, 2 * head_dim), whole)] * 4
            + [pl.BlockSpec((key_block, head_dim), cached)] * 2,
            out_specs=pl.BlockSpec((positions, features), whole),
            scratch_shapes=[
                pltpu.VMEM((row_count, head_dim), jnp.bfloat16),
                pltpu.VMEM((4 * positions, 2 * head_dim), jnp.bfloat16),
                pltpu.VMEM((row_count, head_dim), jnp.float32),
                pltpu.VMEM((row_count, 2 * head_dim), jnp.float32),
            ],
        ),
        out_shape=jax.ShapeDtypeStruct((positions, features), jnp.bfloat16),
        compiler_params=pltpu.CompilerParams(vmem_limit_bytes=VMEM_LIMIT),
        cost_estimate=pl.CostEstimate(
            flops=flops, bytes_accessed=4 * stored * head_dim, transcendentals=row_count * stored
        ),
        name="attend",
    )(prefix_lengths, valid_lengths, query, *fresh, keys, values)


def project_kernel(*refs, adds, outs):
    count = len(adds)
    mine_ref, other_ref = refs[:2]
    w_refs = refs[2 : 2 + count]
    add_refs = refs[2 + count : -outs - 3]
    o_refs = refs[-outs - 3 : -3]
    both, held, arrivals = refs[-3:]
    copies = []
    for index in range(count):
        copy = pltpu.make_async_copy(w_refs[index], held.at[index], arrivals.at[index])
        copy.start()
        copies.append(copy)
    positions = mine_ref.shape[0]
    both[:positions, :] = mine_ref[...]
    both[positions:, :] = other_ref[...]
    pieces, width = held.shape[1], held.shape[3]
    share = count // outs
    for index, copy in enumerate(copies):
        copy.wait()
        o_ref = o_refs[index // share]
        for piece in range(0, pieces, 2):
            tile = jnp.concatenate([held[index, piece], held[index, piece + 1]], axis=1)
            product = jnp.dot(both[...], tile, preferred_element_type=jnp.float32)
            if adds[index] is not None:
                begin = (adds[index] * pieces + piece) * width
                product = product + add_refs[0][:, begin : begin + 2 * width].astype(jnp.float32)
            begin = (index % share * pieces + piece) * width
            o_ref[:, begin : begin + 2 * width] = product.astype(o_ref.dtype)


def project(pair, weights, add=None, added=0, outs=1):
    positions, depth = pair[0].shape
    pieces, _, width = weights[0].shape
    rows = 2 * positions
    count = len(weights)
    columns = count * pieces * width
    covered = 0 if add is None else add.shape[1] // (pieces * width)
    adds = [index - added if added <= index < added + covered else None for index in range(count)]
    whole = pl.BlockSpec(memory_space=pltpu.VMEM)
    return pl.pallas_call(
        functools.partial(project_kernel, adds=adds, outs=outs),
        in_specs=[whole] * 2 + [pl.BlockSpec(memory_space=pl.ANY)] * count + [whole] * (add is not None),
        out_specs=[whole] * outs,
        scratch_shapes=[
            pltpu.VMEM((rows, depth), jnp.bfloat16),
            pltpu.VMEM((count, pieces, depth, width), jnp.bfloat16),
            pltpu.SemaphoreType.DMA((count,)),
        ],
        out_shape=[jax.ShapeDtypeStruct((rows, columns // outs), jnp.bfloat16)] * outs,
        compiler_params=pltpu.CompilerParams(vmem_limit_bytes=VMEM_LIMIT),
        cost_estimate=pl.CostEstimate(
            flops=2 * rows * depth * columns, bytes_accessed=2 * depth * columns, transcendentals=0
        ),
        name="project",
    )(*pair, *weights, *([] if add is None else [add]))


def place_of(row, side):
    chip = lax.div(row, 2)
    return lax.div(chip, side), lax.rem(chip, side)


def combine_kernel(valid_lengths, *refs, groups, width, side):
    o_ref = refs[-1]
    positions = o_ref.shape[1]
    start = lax.axis_index("sp") * positions
    row = lax.axis_index("dp")
    core = lax.rem(row, 2)
    y, z = place_of(row, side)
    keep = start + lax.broadcasted_iota(jnp.int32, (positions, width), 0) < valid_lengths[row]
    for part, members in enumerate(groups):
        own, first, second, arrived = refs[4 * part : 4 * part + 4]
        for index, (kind, offset) in enumerate(members):
            for step in range(side):
                dy, dz = (step, offset) if kind == 0 else (offset, step)
                piece = lax.rem(y + dy, side) * side + lax.rem(z + dz, side)
                columns = slice((index * side + step) * width, (index * side + step + 1) * width)
                total = (
                    own[:, columns].astype(jnp.float32)
                    + first[:, columns].astype(jnp.float32)
                    + second[:, columns].astype(jnp.float32)
                )
                for source, value in ((core, total.astype(o_ref.dtype)), (1 - core, arrived[:, columns])):
                    column = pl.multiple_of((2 * piece + source) * 2 * width + kind * width, width)
                    o_ref[0, :, pl.ds(column, width)] = jnp.where(keep, value, jnp.zeros_like(value))


def combine(valid_lengths, parts, groups, positions, width, side):
    columns = 4 * width * side * side
    return pl.pallas_call(
        functools.partial(combine_kernel, groups=groups, width=width, side=side),
        grid_spec=pltpu.PrefetchScalarGridSpec(
            num_scalar_prefetch=1,
            grid=(1,),
            in_specs=[pl.BlockSpec((positions, part.shape[1]), lambda step, _: (0, 0)) for part in parts],
            out_specs=pl.BlockSpec((1, positions, columns), lambda step, _: (0, 0, 0)),
        ),
        out_shape=jax.ShapeDtypeStruct((1, positions, columns), jnp.bfloat16),
        compiler_params=pltpu.CompilerParams(vmem_limit_bytes=VMEM_LIMIT),
        name="combine",
    )(valid_lengths, *parts)


def local(
    queries,
    rotated_span_keys,
    span_value_heads,
    cache_keys,
    cached_prefix_values,
    out_weight,
    prefix_lengths,
    valid_lengths,
):
    parts = lax.axis_size("sp")
    rows = lax.axis_size("dp")
    me = lax.axis_index("sp")
    positions = queries.shape[1]
    head_dim = cache_keys.shape[3]
    features = queries.shape[2] // parts

    side = math.isqrt(rows // 2)
    width = out_weight.shape[1] // 2

    def shift(array, distance):
        return lax.ppermute(array, "sp", [(i, (i + distance) % parts) for i in range(parts)])

    def swap(array):
        return lax.ppermute(array, "dp", [(i, i ^ 1) for i in range(rows)])

    def across(array, dy, dz):
        pairs = []
        for i in range(rows):
            y, z, core = i // (2 * side), (i // 2) % side, i % 2
            pairs.append((i, (((y + dy) % side) * side + (z + dz) % side) * 2 + core))
        return lax.ppermute(array, "dp", pairs)

    def after(value, *others):
        return lax.optimization_barrier((value, *others))[0]

    def part_of(array, owner, size):
        return lax.dynamic_slice_in_dim(array, owner * size, size, 1)

    def gather_line(piece, dy, dz):
        return [piece, across(piece, -dy, -dz), across(piece, 2 * dy, 2 * dz), across(piece, dy, dz)]

    pieces = [out_weight[:, :width], out_weight[:, width:]]
    lines = [gather_line(pieces[0], 1, 0), gather_line(pieces[1], 0, 1)]
    fresh, query = [None] * parts, [None] * parts
    for distance in (2, 1, 3, 0):
        owner = lax.rem(me + distance, parts)
        pair = jnp.concatenate(
            [part_of(rotated_span_keys[0], owner, head_dim), part_of(span_value_heads[0], owner, head_dim)], axis=1
        )
        fresh[(parts - distance) % parts] = shift(pair, distance) if distance else pair
    for distance in (3, 2, 1, 0):
        part = part_of(queries[0], lax.rem(me + distance, parts), features)
        query[(parts - distance) % parts] = shift(part, distance) if distance else part

    def attended(distance, *waits):
        mine = attend(
            prefix_lengths,
            valid_lengths,
            after(query[distance], *waits),
            fresh,
            distance,
            cache_keys[0, 0],
            cached_prefix_values[0, 0],
        )
        return mine, swap(mine)

    lines = [jnp.stack(line) for line in lines]
    behind = [across(lines[0], 0, 1), across(lines[1], 1, 0)]
    ahead = [across(lines[0], 0, -1), across(lines[1], -1, 0)]
    right = attended(1, *lines)
    far = attended(2, right[0])
    half = side // 2
    behind_part = [after(array[:half], far[0]) for array in behind]
    ahead_part = [after(array[half:], far[0]) for array in ahead]
    opposite = [
        [across(behind_part[0], 0, 1), across(ahead_part[0], 0, -1)],
        [across(behind_part[1], 1, 0), across(ahead_part[1], -1, 0)],
    ]
    early = [lines[0], ahead[0], behind[0], lines[1], ahead[1], behind[1]]
    early_groups = [(0, 0), (0, 1), (0, 3), (1, 0), (1, 1), (1, 3)]
    late_groups = [(0, 2), (1, 2)]

    far_right, far_left = project(far, early, outs=2)
    from_left, from_right = shift(far_right, 1), shift(far_left, -1)
    left = attended(3, far_right, *behind_part, *ahead_part)
    opposite = [jnp.concatenate([after(array, left[0]) for array in arrays], axis=0) for arrays in opposite]
    far_right, far_left = project(far, opposite, outs=2)
    from_left_late, from_right_late = shift(far_right, 1), shift(far_left, -1)
    (right_early,) = project(right, early, after(from_left, far_right), 0)
    (left_early,) = project(left, early, after(from_right, far_right), 3)
    right_in, left_in = shift(right_early, 1), shift(left_early, -1)
    (right_late,) = project(right, opposite, after(from_left_late, right_early, left_early), 0)
    (left_late,) = project(left, opposite, after(from_right_late, right_early, left_early), 1)
    right_late_in, left_late_in = shift(right_late, 1), shift(left_late, -1)
    own = attended(0, left_late, right_late)
    (own_early,) = project(own, early)
    (own_late,) = project(own, opposite)

    def summed(*terms):
        return sum(term[positions:].astype(jnp.float32) for term in terms).astype(jnp.bfloat16)

    early_terms = (own_early, right_in, left_in)
    late_terms = (own_late, right_late_in, left_late_in)
    return combine(
        valid_lengths,
        [*early_terms, swap(summed(*early_terms)), *late_terms, swap(summed(*late_terms))],
        [early_groups, late_groups],
        positions,
        width,
        side,
    )


def solution(mesh):
    in_specs = (
        P("dp", "sp", None),
        P("dp", "sp", None),
        P("dp", "sp", None),
        P("dp", "sp", None, None),
        P("dp", "sp", None, None),
        P("sp", "dp"),
        P(),
        P(),
    )
    out_specs = P("dp", "sp", None)
    return jax.shard_map(local, mesh=mesh, in_specs=in_specs, out_specs=out_specs, check_vma=False)
```

```python
import functools
import math

import jax
import jax.numpy as jnp
from jax import lax
from jax.experimental import pallas as pl
from jax.experimental.pallas import tpu as pltpu
from jax.sharding import PartitionSpec as P

NEGATIVE = -1e30
VMEM_LIMIT = 48 << 20
KEY_BLOCK = 4096
KEY_PIECE = 1024
ROW_CHUNK = 128


def attention_kernel(
    prefix_lengths,
    valid_lengths,
    q_ref,
    s0_ref,
    s1_ref,
    s2_ref,
    s3_ref,
    k_ref,
    v_ref,
    o_ref,
    rows,
    span,
    high,
    total,
    *,
    distance,
    factor,
):
    step = pl.program_id(0)
    head_dim = k_ref.shape[1]
    positions = q_ref.shape[0]
    heads = o_ref.shape[1] // head_dim
    row_count = heads * positions
    key_block = k_ref.shape[0]
    chunk = min(ROW_CHUNK, row_count)
    parts = lax.axis_size("sp")
    me = lax.axis_index("sp")
    row = lax.axis_index("dp")
    length = prefix_lengths[row]

    def start_of(offset):
        return lax.rem(me + offset, parts) * positions

    first_position = start_of(distance)
    live = first_position < valid_lengths[row]

    def update(keys, values, usable):
        augmented = jnp.concatenate([values, jnp.ones_like(values)], axis=1)

        def score(start):
            return lax.dot_general(
                rows[pl.ds(start, chunk), :],
                keys,
                (((1,), (1,)), ((), ())),
                preferred_element_type=jnp.float32,
            )

        def fold(start, scores):
            if usable is not None:
                scores = jnp.where(usable(scores.shape), scores, NEGATIVE)
            block = pl.ds(start, chunk)
            before = high[block, :]
            after = jnp.maximum(before, jnp.max(scores, axis=1, keepdims=True))
            high[block, :] = after
            rescale = jnp.exp2((before - after) * factor)
            weights = jnp.exp2((scores - after[:, :1]) * factor).astype(jnp.bfloat16)
            total[block, :] = total[block, :] * jnp.concatenate([rescale, rescale], axis=1) + jnp.dot(
                weights, augmented, preferred_element_type=jnp.float32
            )

        following = score(0)
        for start in range(0, row_count, chunk):
            scores = following
            if start + chunk < row_count:
                following = score(start + chunk)
            fold(start, scores)

    @pl.when(jnp.logical_and(step == 0, live))
    def _():
        for head in range(heads):
            rows[head * positions : (head + 1) * positions, :] = q_ref[:, head * head_dim : (head + 1) * head_dim]
        high[...] = jnp.full_like(high, NEGATIVE)
        total[...] = jnp.zeros_like(total)
        for index, source in enumerate((s0_ref, s1_ref, s2_ref, s3_ref)):
            span[index * positions : (index + 1) * positions, :] = source[...]

        def causal(shape):
            query = first_position + lax.rem(lax.broadcasted_iota(jnp.int32, shape, 0), positions)
            column = lax.broadcasted_iota(jnp.int32, shape, 1)
            key = start_of(0) + column
            for index in range(1, parts):
                key = jnp.where(column >= index * positions, start_of(index) + column - index * positions, key)
            return key <= query

        update(span[:, :head_dim], span[:, head_dim:], causal)

    before_block = (step - 1) * key_block

    @pl.when(jnp.logical_and(live, jnp.logical_and(step > 0, step * key_block <= length)))
    def _():
        update(k_ref[...], v_ref[...], None)

    @pl.when(
        jnp.logical_and(
            live,
            jnp.logical_and(step > 0, jnp.logical_and(before_block < length, step * key_block > length)),
        )
    )
    def _():
        piece = math.gcd(KEY_PIECE, key_block)

        @pl.loop(0, lax.div(length - before_block + piece - 1, piece))
        def _(index):
            begin = pl.multiple_of(index * piece, piece)

            def stored(shape):
                return before_block + begin + lax.broadcasted_iota(jnp.int32, shape, 1) < length

            update(k_ref[pl.ds(begin, piece), :], v_ref[pl.ds(begin, piece), :], stored)

    @pl.when(step == pl.num_programs(0) - 1)
    def _():
        @pl.when(live)
        def _():
            for head in range(heads):
                block = slice(head * positions, (head + 1) * positions)
                o_ref[:, head * head_dim : (head + 1) * head_dim] = (
                    total[block, :head_dim] / total[block, head_dim:]
                ).astype(o_ref.dtype)

        @pl.when(jnp.logical_not(live))
        def _():
            o_ref[...] = jnp.zeros_like(o_ref)


def attend(prefix_lengths, valid_lengths, query, fresh, distance, keys, values):
    positions, features = query.shape
    stored, head_dim = keys.shape
    key_block = math.gcd(KEY_BLOCK, stored)
    count = stored // key_block
    row_count = positions * features // head_dim

    def cached(step, prefix_lengths, valid_lengths):
        last = lax.div(prefix_lengths[lax.axis_index("dp")] - 1, key_block)
        return (jnp.clip(step - 1, 0, last), 0)

    def whole(step, *_):
        return (0, 0)

    flops = 8 * row_count * (stored + 4 * positions) * head_dim
    return pl.pallas_call(
        functools.partial(attention_kernel, distance=distance, factor=math.log2(math.e) / math.sqrt(head_dim)),
        grid_spec=pltpu.PrefetchScalarGridSpec(
            num_scalar_prefetch=2,
            grid=(count + 1,),
            in_specs=[pl.BlockSpec((positions, features), whole)]
            + [pl.BlockSpec((positions, 2 * head_dim), whole)] * 4
            + [pl.BlockSpec((key_block, head_dim), cached)] * 2,
            out_specs=pl.BlockSpec((positions, features), whole),
            scratch_shapes=[
                pltpu.VMEM((row_count, head_dim), jnp.bfloat16),
                pltpu.VMEM((4 * positions, 2 * head_dim), jnp.bfloat16),
                pltpu.VMEM((row_count, head_dim), jnp.float32),
                pltpu.VMEM((row_count, 2 * head_dim), jnp.float32),
            ],
        ),
        out_shape=jax.ShapeDtypeStruct((positions, features), jnp.bfloat16),
        compiler_params=pltpu.CompilerParams(vmem_limit_bytes=VMEM_LIMIT),
        cost_estimate=pl.CostEstimate(
            flops=flops, bytes_accessed=4 * stored * head_dim, transcendentals=row_count * stored
        ),
        name="attend",
    )(prefix_lengths, valid_lengths, query, *fresh, keys, values)


def project_kernel(*refs, adds, outs):
    count = len(adds)
    mine_ref, other_ref = refs[:2]
    w_refs = refs[2 : 2 + count]
    add_refs = refs[2 + count : -outs - 3]
    o_refs = refs[-outs - 3 : -3]
    both, held, arrivals = refs[-3:]
    copies = []
    for index in range(count):
        copy = pltpu.make_async_copy(w_refs[index], held.at[index], arrivals.at[index])
        copy.start()
        copies.append(copy)
    positions = mine_ref.shape[0]
    both[:positions, :] = mine_ref[...]
    both[positions:, :] = other_ref[...]
    pieces, width = held.shape[1], held.shape[3]
    share = count // outs
    for index, copy in enumerate(copies):
        copy.wait()
        o_ref = o_refs[index // share]
        for piece in range(0, pieces, 2):
            tile = jnp.concatenate([held[index, piece], held[index, piece + 1]], axis=1)
            product = jnp.dot(both[...], tile, preferred_element_type=jnp.float32)
            if adds[index] is not None:
                begin = (adds[index] * pieces + piece) * width
                product = product + add_refs[0][:, begin : begin + 2 * width].astype(jnp.float32)
            begin = (index % share * pieces + piece) * width
            o_ref[:, begin : begin + 2 * width] = product.astype(o_ref.dtype)


def project(pair, weights, add=None, added=0, outs=1):
    positions, depth = pair[0].shape
    pieces, _, width = weights[0].shape
    rows = 2 * positions
    count = len(weights)
    columns = count * pieces * width
    covered = 0 if add is None else add.shape[1] // (pieces * width)
    adds = [index - added if added <= index < added + covered else None for index in range(count)]
    whole = pl.BlockSpec(memory_space=pltpu.VMEM)
    return pl.pallas_call(
        functools.partial(project_kernel, adds=adds, outs=outs),
        in_specs=[whole] * 2 + [pl.BlockSpec(memory_space=pl.ANY)] * count + [whole] * (add is not None),
        out_specs=[whole] * outs,
        scratch_shapes=[
            pltpu.VMEM((rows, depth), jnp.bfloat16),
            pltpu.VMEM((count, pieces, depth, width), jnp.bfloat16),
            pltpu.SemaphoreType.DMA((count,)),
        ],
        out_shape=[jax.ShapeDtypeStruct((rows, columns // outs), jnp.bfloat16)] * outs,
        compiler_params=pltpu.CompilerParams(vmem_limit_bytes=VMEM_LIMIT),
        cost_estimate=pl.CostEstimate(
            flops=2 * rows * depth * columns, bytes_accessed=2 * depth * columns, transcendentals=0
        ),
        name="project",
    )(*pair, *weights, *([] if add is None else [add]))


def place_of(row, side):
    chip = lax.div(row, 2)
    return lax.div(chip, side), lax.rem(chip, side)


def combine_kernel(valid_lengths, *refs, groups, width, side):
    o_ref = refs[-1]
    positions = o_ref.shape[1]
    start = lax.axis_index("sp") * positions
    row = lax.axis_index("dp")
    core = lax.rem(row, 2)
    y, z = place_of(row, side)
    keep = start + lax.broadcasted_iota(jnp.int32, (positions, width), 0) < valid_lengths[row]
    for part, members in enumerate(groups):
        own, first, second, arrived = refs[4 * part : 4 * part + 4]
        for index, (kind, offset) in enumerate(members):
            for step in range(side):
                dy, dz = (step, offset) if kind == 0 else (offset, step)
                piece = lax.rem(y + dy, side) * side + lax.rem(z + dz, side)
                columns = slice((index * side + step) * width, (index * side + step + 1) * width)
                total = (
                    own[:, columns].astype(jnp.float32)
                    + first[:, columns].astype(jnp.float32)
                    + second[:, columns].astype(jnp.float32)
                )
                for source, value in ((core, total.astype(o_ref.dtype)), (1 - core, arrived[:, columns])):
                    column = pl.multiple_of((2 * piece + source) * 2 * width + kind * width, width)
                    o_ref[0, :, pl.ds(column, width)] = jnp.where(keep, value, jnp.zeros_like(value))


def combine(valid_lengths, parts, groups, positions, width, side):
    columns = 4 * width * side * side
    return pl.pallas_call(
        functools.partial(combine_kernel, groups=groups, width=width, side=side),
        grid_spec=pltpu.PrefetchScalarGridSpec(
            num_scalar_prefetch=1,
            grid=(1,),
            in_specs=[pl.BlockSpec((positions, part.shape[1]), lambda step, _: (0, 0)) for part in parts],
            out_specs=pl.BlockSpec((1, positions, columns), lambda step, _: (0, 0, 0)),
        ),
        out_shape=jax.ShapeDtypeStruct((1, positions, columns), jnp.bfloat16),
        compiler_params=pltpu.CompilerParams(vmem_limit_bytes=VMEM_LIMIT),
        name="combine",
    )(valid_lengths, *parts)


def local(
    queries,
    rotated_span_keys,
    span_value_heads,
    cache_keys,
    cached_prefix_values,
    out_weight,
    prefix_lengths,
    valid_lengths,
):
    parts = lax.axis_size("sp")
    rows = lax.axis_size("dp")
    me = lax.axis_index("sp")
    positions = queries.shape[1]
    head_dim = cache_keys.shape[3]
    features = queries.shape[2] // parts

    side = math.isqrt(rows // 2)
    width = out_weight.shape[1] // 2

    def shift(array, distance):
        return lax.ppermute(array, "sp", [(i, (i + distance) % parts) for i in range(parts)])

    def swap(array):
        return lax.ppermute(array, "dp", [(i, i ^ 1) for i in range(rows)])

    def across(array, dy, dz):
        pairs = []
        for i in range(rows):
            y, z, core = i // (2 * side), (i // 2) % side, i % 2
            pairs.append((i, (((y + dy) % side) * side + (z + dz) % side) * 2 + core))
        return lax.ppermute(array, "dp", pairs)

    def after(value, *others):
        return lax.optimization_barrier((value, *others))[0]

    def part_of(array, owner, size):
        return lax.dynamic_slice_in_dim(array, owner * size, size, 1)

    def gather_line(piece, dy, dz):
        return [piece, across(piece, -dy, -dz), across(piece, 2 * dy, 2 * dz), across(piece, dy, dz)]

    pieces = [out_weight[:, :width], out_weight[:, width:]]
    lines = [gather_line(pieces[0], 1, 0), gather_line(pieces[1], 0, 1)]
    fresh, query = [None] * parts, [None] * parts
    for distance in (2, 1, 3, 0):
        owner = lax.rem(me + distance, parts)
        pair = jnp.concatenate(
            [part_of(rotated_span_keys[0], owner, head_dim), part_of(span_value_heads[0], owner, head_dim)], axis=1
        )
        fresh[(parts - distance) % parts] = shift(pair, distance) if distance else pair
    for distance in (3, 2, 1, 0):
        part = part_of(queries[0], lax.rem(me + distance, parts), features)
        query[(parts - distance) % parts] = shift(part, distance) if distance else part

    def attended(distance, *waits):
        mine = attend(
            prefix_lengths,
            valid_lengths,
            after(query[distance], *waits),
            fresh,
            distance,
            cache_keys[0, 0],
            cached_prefix_values[0, 0],
        )
        return mine, swap(mine)

    lines = [jnp.stack(line) for line in lines]
    behind = [across(lines[0], 0, 1), across(lines[1], 1, 0)]
    ahead = [across(lines[0], 0, -1), across(lines[1], -1, 0)]
    right = attended(1, *lines)
    far = attended(2, right[0])
    half = side // 2
    early = [lines[0], ahead[0], behind[0], lines[1], ahead[1], behind[1]]
    early_groups = [(0, 0), (0, 1), (0, 3), (1, 0), (1, 1), (1, 3)]
    late_groups = [(0, 2), (1, 2)]

    first_behind, first_ahead = after(behind[0][:half], far[0]), after(ahead[0][half:], far[0])
    opposite = [[across(first_behind, 0, 1), across(first_ahead, 0, -1)]]
    far_right, far_left = project((after(far[0], first_behind, first_ahead), far[1]), early, outs=2)
    from_left, from_right = shift(far_right, 1), shift(far_left, -1)
    second_behind, second_ahead = after(behind[1][:half], far_right), after(ahead[1][half:], far_right)
    opposite.append([across(second_behind, 1, 0), across(second_ahead, -1, 0)])
    left = attended(3, far_right, second_behind, second_ahead)
    opposite = [jnp.concatenate([after(array, left[0]) for array in arrays], axis=0) for arrays in opposite]
    far_right, far_left = project(far, opposite, outs=2)
    from_left_late, from_right_late = shift(far_right, 1), shift(far_left, -1)
    (right_early,) = project(right, early, after(from_left, far_right), 0)
    (left_early,) = project(left, early, after(from_right, far_right), 3)
    right_in, left_in = shift(right_early, 1), shift(left_early, -1)
    (right_late,) = project(right, opposite, after(from_left_late, right_early, left_early), 0)
    (left_late,) = project(left, opposite, after(from_right_late, right_early, left_early), 1)
    right_late_in, left_late_in = shift(right_late, 1), shift(left_late, -1)
    own = attended(0, left_late, right_late)
    (own_early,) = project(own, early)
    (own_late,) = project(own, opposite)

    def summed(*terms):
        return sum(term[positions:].astype(jnp.float32) for term in terms).astype(jnp.bfloat16)

    early_terms = (own_early, right_in, left_in)
    late_terms = (own_late, right_late_in, left_late_in)
    return combine(
        valid_lengths,
        [*early_terms, swap(summed(*early_terms)), *late_terms, swap(summed(*late_terms))],
        [early_groups, late_groups],
        positions,
        width,
        side,
    )


def solution(mesh):
    in_specs = (
        P("dp", "sp", None),
        P("dp", "sp", None),
        P("dp", "sp", None),
        P("dp", "sp", None, None),
        P("dp", "sp", None, None),
        P("sp", "dp"),
        P(),
        P(),
    )
    out_specs = P("dp", "sp", None)
    return jax.shard_map(local, mesh=mesh, in_specs=in_specs, out_specs=out_specs, check_vma=False)
```

```python
import functools
import math

import jax
import jax.numpy as jnp
from jax import lax
from jax.experimental import pallas as pl
from jax.experimental.pallas import tpu as pltpu
from jax.sharding import PartitionSpec as P

NEGATIVE = -1e30
VMEM_LIMIT = 48 << 20
KEY_BLOCK = 4096
KEY_PIECE = 1024
ROW_CHUNK = 128


def trajectory(sibling):
    row = lax.axis_index("dp")
    return row + 1 - 2 * lax.rem(row, 2) if sibling else row


def attention_kernel(
    prefix_lengths,
    valid_lengths,
    q_ref,
    span_ref,
    k_ref,
    v_ref,
    o_ref,
    rows,
    high,
    total,
    *,
    distance,
    sibling,
    factor,
):
    step = pl.program_id(0)
    head_dim = k_ref.shape[1]
    positions = q_ref.shape[0]
    heads = o_ref.shape[1] // head_dim
    row_count = heads * positions
    key_block = k_ref.shape[0]
    chunk = min(ROW_CHUNK, row_count)
    parts = lax.axis_size("sp")
    me = lax.axis_index("sp")
    row = trajectory(sibling)
    length = prefix_lengths[row]

    def start_of(offset):
        return lax.rem(me + offset, parts) * positions

    first_position = start_of(distance)
    live = first_position < valid_lengths[row]

    def update(keys, values, usable):
        augmented = jnp.concatenate([values, jnp.ones_like(values)], axis=1)

        def score(start):
            return lax.dot_general(
                rows[pl.ds(start, chunk), :],
                keys,
                (((1,), (1,)), ((), ())),
                preferred_element_type=jnp.float32,
            )

        def fold(start, scores):
            if usable is not None:
                scores = jnp.where(usable(scores.shape), scores, NEGATIVE)
            block = pl.ds(start, chunk)
            before = high[block, :]
            after = jnp.maximum(before, jnp.max(scores, axis=1, keepdims=True))
            high[block, :] = after
            rescale = jnp.exp2((before - after) * factor)
            weights = jnp.exp2((scores - after[:, :1]) * factor).astype(jnp.bfloat16)
            total[block, :] = total[block, :] * jnp.concatenate([rescale, rescale], axis=1) + jnp.dot(
                weights, augmented, preferred_element_type=jnp.float32
            )

        following = score(0)
        for start in range(0, row_count, chunk):
            scores = following
            if start + chunk < row_count:
                following = score(start + chunk)
            fold(start, scores)

    @pl.when(jnp.logical_and(step == 0, live))
    def _():
        for head in range(heads):
            rows[head * positions : (head + 1) * positions, :] = q_ref[:, head * head_dim : (head + 1) * head_dim]
        high[...] = jnp.full_like(high, NEGATIVE)
        total[...] = jnp.zeros_like(total)

        def causal(shape):
            query = first_position + lax.rem(lax.broadcasted_iota(jnp.int32, shape, 0), positions)
            column = lax.broadcasted_iota(jnp.int32, shape, 1)
            key = start_of(0) + column
            for index in range(1, parts):
                key = jnp.where(column >= index * positions, start_of(index) + column - index * positions, key)
            return key <= query

        update(span_ref[:, :head_dim], span_ref[:, head_dim:], causal)

    before_block = (step - 1) * key_block

    @pl.when(jnp.logical_and(live, jnp.logical_and(step > 0, step * key_block <= length)))
    def _():
        update(k_ref[...], v_ref[...], None)

    @pl.when(
        jnp.logical_and(
            live,
            jnp.logical_and(step > 0, jnp.logical_and(before_block < length, step * key_block > length)),
        )
    )
    def _():
        piece = math.gcd(KEY_PIECE, key_block)

        @pl.loop(0, lax.div(length - before_block + piece - 1, piece))
        def _(index):
            begin = pl.multiple_of(index * piece, piece)

            def stored(shape):
                return before_block + begin + lax.broadcasted_iota(jnp.int32, shape, 1) < length

            update(k_ref[pl.ds(begin, piece), :], v_ref[pl.ds(begin, piece), :], stored)

    @pl.when(step == pl.num_programs(0) - 1)
    def _():
        @pl.when(live)
        def _():
            for head in range(heads):
                block = slice(head * positions, (head + 1) * positions)
                o_ref[:, head * head_dim : (head + 1) * head_dim] = (
                    total[block, :head_dim] / total[block, head_dim:]
                ).astype(o_ref.dtype)

        @pl.when(jnp.logical_not(live))
        def _():
            o_ref[...] = jnp.zeros_like(o_ref)


def attend(prefix_lengths, valid_lengths, query, fresh, distance, sibling, keys, values):
    positions, features = query.shape
    stored, head_dim = keys.shape
    key_block = math.gcd(KEY_BLOCK, stored)
    count = stored // key_block
    row_count = positions * features // head_dim

    def cached(step, prefix_lengths, valid_lengths):
        last = lax.div(prefix_lengths[trajectory(sibling)] - 1, key_block)
        return (jnp.clip(step - 1, 0, last), 0)

    def whole(step, *_):
        return (0, 0)

    flops = 8 * row_count * (stored + fresh.shape[0]) * head_dim
    return pl.pallas_call(
        functools.partial(
            attention_kernel, distance=distance, sibling=sibling, factor=math.log2(math.e) / math.sqrt(head_dim)
        ),
        grid_spec=pltpu.PrefetchScalarGridSpec(
            num_scalar_prefetch=2,
            grid=(count + 1,),
            in_specs=[pl.BlockSpec((positions, features), whole)]
            + [pl.BlockSpec(fresh.shape, whole)]
            + [pl.BlockSpec((key_block, head_dim), cached)] * 2,
            out_specs=pl.BlockSpec((positions, features), whole),
            scratch_shapes=[
                pltpu.VMEM((row_count, head_dim), jnp.bfloat16),
                pltpu.VMEM((row_count, head_dim), jnp.float32),
                pltpu.VMEM((row_count, 2 * head_dim), jnp.float32),
            ],
        ),
        out_shape=jax.ShapeDtypeStruct((positions, features), jnp.bfloat16),
        compiler_params=pltpu.CompilerParams(vmem_limit_bytes=VMEM_LIMIT),
        cost_estimate=pl.CostEstimate(
            flops=flops, bytes_accessed=4 * stored * head_dim, transcendentals=row_count * stored
        ),
        name="attend",
    )(prefix_lengths, valid_lengths, query, fresh, keys, values)


def project_kernel(*refs, adds, outs):
    count = len(adds)
    mine_ref, other_ref = refs[:2]
    w_refs = refs[2 : 2 + count]
    add_refs = refs[2 + count : -outs - 3]
    o_refs = refs[-outs - 3 : -3]
    both, held, arrivals = refs[-3:]
    copies = []
    for index in range(count):
        copy = pltpu.make_async_copy(w_refs[index], held.at[index], arrivals.at[index])
        copy.start()
        copies.append(copy)
    positions = mine_ref.shape[0]
    both[:positions, :] = mine_ref[...]
    both[positions:, :] = other_ref[...]
    pieces, width = held.shape[1], held.shape[3]
    share = count // outs
    for index, copy in enumerate(copies):
        copy.wait()
        o_ref = o_refs[index // share]
        for piece in range(0, pieces, 2):
            tile = jnp.concatenate([held[index, piece], held[index, piece + 1]], axis=1)
            product = jnp.dot(both[...], tile, preferred_element_type=jnp.float32)
            if adds[index] is not None:
                begin = (adds[index] * pieces + piece) * width
                product = product + add_refs[0][:, begin : begin + 2 * width].astype(jnp.float32)
            begin = (index % share * pieces + piece) * width
            o_ref[:, begin : begin + 2 * width] = product.astype(o_ref.dtype)


def project(pair, weights, add=None, added=0, outs=1):
    positions, depth = pair[0].shape
    pieces, _, width = weights[0].shape
    rows = 2 * positions
    count = len(weights)
    columns = count * pieces * width
    covered = 0 if add is None else add.shape[1] // (pieces * width)
    adds = [index - added if added <= index < added + covered else None for index in range(count)]
    whole = pl.BlockSpec(memory_space=pltpu.VMEM)
    return pl.pallas_call(
        functools.partial(project_kernel, adds=adds, outs=outs),
        in_specs=[whole] * 2 + [pl.BlockSpec(memory_space=pl.ANY)] * count + [whole] * (add is not None),
        out_specs=[whole] * outs,
        scratch_shapes=[
            pltpu.VMEM((rows, depth), jnp.bfloat16),
            pltpu.VMEM((count, pieces, depth, width), jnp.bfloat16),
            pltpu.SemaphoreType.DMA((count,)),
        ],
        out_shape=[jax.ShapeDtypeStruct((rows, columns // outs), jnp.bfloat16)] * outs,
        compiler_params=pltpu.CompilerParams(vmem_limit_bytes=VMEM_LIMIT),
        cost_estimate=pl.CostEstimate(
            flops=2 * rows * depth * columns, bytes_accessed=2 * depth * columns, transcendentals=0
        ),
        name="project",
    )(*pair, *weights, *([] if add is None else [add]))


def place_of(row, side):
    chip = lax.div(row, 2)
    return lax.div(chip, side), lax.rem(chip, side)


def combine_kernel(valid_lengths, *refs, groups, width, side):
    o_ref = refs[-1]
    positions = o_ref.shape[1]
    start = lax.axis_index("sp") * positions
    row = lax.axis_index("dp")
    core = lax.rem(row, 2)
    y, z = place_of(row, side)
    keep = start + lax.broadcasted_iota(jnp.int32, (positions, width), 0) < valid_lengths[row]
    for part, members in enumerate(groups):
        own, first, second, arrived = refs[4 * part : 4 * part + 4]
        for index, (kind, offset) in enumerate(members):
            for step in range(side):
                dy, dz = (step, offset) if kind == 0 else (offset, step)
                piece = lax.rem(y + dy, side) * side + lax.rem(z + dz, side)
                columns = slice((index * side + step) * width, (index * side + step + 1) * width)
                total = (
                    own[:, columns].astype(jnp.float32)
                    + first[:, columns].astype(jnp.float32)
                    + second[:, columns].astype(jnp.float32)
                )
                for source, value in ((core, total.astype(o_ref.dtype)), (1 - core, arrived[:, columns])):
                    column = pl.multiple_of((2 * piece + source) * 2 * width + kind * width, width)
                    o_ref[0, :, pl.ds(column, width)] = jnp.where(keep, value, jnp.zeros_like(value))


def combine(valid_lengths, parts, groups, positions, width, side):
    columns = 4 * width * side * side
    return pl.pallas_call(
        functools.partial(combine_kernel, groups=groups, width=width, side=side),
        grid_spec=pltpu.PrefetchScalarGridSpec(
            num_scalar_prefetch=1,
            grid=(1,),
            in_specs=[pl.BlockSpec((positions, part.shape[1]), lambda step, _: (0, 0)) for part in parts],
            out_specs=pl.BlockSpec((1, positions, columns), lambda step, _: (0, 0, 0)),
        ),
        out_shape=jax.ShapeDtypeStruct((1, positions, columns), jnp.bfloat16),
        compiler_params=pltpu.CompilerParams(vmem_limit_bytes=VMEM_LIMIT),
        name="combine",
    )(valid_lengths, *parts)


def local(
    queries,
    rotated_span_keys,
    span_value_heads,
    cache_keys,
    cached_prefix_values,
    out_weight,
    prefix_lengths,
    valid_lengths,
):
    parts = lax.axis_size("sp")
    rows = lax.axis_size("dp")
    me = lax.axis_index("sp")
    positions = queries.shape[1]
    head_dim = cache_keys.shape[3]
    features = queries.shape[2] // parts

    side = math.isqrt(rows // 2)
    width = out_weight.shape[1] // 2

    def shift(array, distance):
        return lax.ppermute(array, "sp", [(i, (i + distance) % parts) for i in range(parts)])

    def swap(array):
        return lax.ppermute(array, "dp", [(i, i ^ 1) for i in range(rows)])

    def across(array, dy, dz):
        pairs = []
        for i in range(rows):
            y, z, core = i // (2 * side), (i // 2) % side, i % 2
            pairs.append((i, (((y + dy) % side) * side + (z + dz) % side) * 2 + core))
        return lax.ppermute(array, "dp", pairs)

    def after(value, *others):
        return lax.optimization_barrier((value, *others))[0]

    def part_of(array, owner, size):
        return lax.dynamic_slice_in_dim(array, owner * size, size, 1)

    def gather_line(piece, dy, dz):
        return [piece, across(piece, -dy, -dz), across(piece, 2 * dy, 2 * dz), across(piece, dy, dz)]

    pieces = [out_weight[:, :width], out_weight[:, width:]]
    lines = [gather_line(pieces[0], 1, 0), gather_line(pieces[1], 0, 1)]
    def shift_across(array, distance):
        pairs = [
            (row * parts + i, (row ^ 1) * parts + (i + distance) % parts) for row in range(rows) for i in range(parts)
        ]
        return lax.ppermute(array, ("dp", "sp"), pairs)

    fresh, query = [None] * parts, [None] * parts
    for distance in (2, 1, 3, 0):
        owner = lax.rem(me + distance, parts)
        pair = jnp.concatenate(
            [part_of(rotated_span_keys[0], owner, head_dim), part_of(span_value_heads[0], owner, head_dim)], axis=1
        )
        fresh[(parts - distance) % parts] = shift(pair, distance) if distance else pair
    for distance in (3, 2, 1, 0):
        part = part_of(queries[0], lax.rem(me + distance, parts), features)
        if distance == 0:
            query[0] = swap(part)
        elif distance == 2:
            query[2] = shift_across(part, distance)
        else:
            query[parts - distance] = shift(part, distance)
    fresh = jnp.concatenate(fresh, axis=0)
    keys, values = cache_keys[0, 0], cached_prefix_values[0, 0]
    stores = {False: (fresh, keys, values), True: (swap(fresh), swap(keys), swap(values))}

    def attended(distance, *waits):
        sibling = distance % 2 == 0
        fresh, keys, values = stores[sibling]
        result = attend(
            prefix_lengths,
            valid_lengths,
            after(query[distance], *waits),
            fresh,
            distance,
            sibling,
            keys,
            values,
        )
        return result, swap(result)

    def mine_first(distance, pair):
        return pair[::-1] if distance % 2 == 0 else pair

    lines = [jnp.stack(line) for line in lines]
    behind = [across(lines[0], 0, 1), across(lines[1], 1, 0)]
    ahead = [across(lines[0], 0, -1), across(lines[1], -1, 0)]
    right = attended(1, *lines)
    far = attended(2, right[0])
    half = side // 2
    early = [lines[0], ahead[0], behind[0], lines[1], ahead[1], behind[1]]
    early_groups = [(0, 0), (0, 1), (0, 3), (1, 0), (1, 1), (1, 3)]
    late_groups = [(0, 2), (1, 2)]

    first_behind, first_ahead = after(behind[0][:half], far[0]), after(ahead[0][half:], far[0])
    opposite = [[across(first_behind, 0, 1), across(first_ahead, 0, -1)]]
    far = mine_first(2, (after(far[0], first_behind, first_ahead), far[1]))
    far_right, far_left = project(far, early, outs=2)
    from_left, from_right = shift(far_right, 1), shift(far_left, -1)
    second_behind, second_ahead = after(behind[1][:half], far_right), after(ahead[1][half:], far_right)
    opposite.append([across(second_behind, 1, 0), across(second_ahead, -1, 0)])
    left = attended(3, far_right, second_behind, second_ahead)
    own = attended(0, left[0])
    opposite = [jnp.concatenate([after(array, own[0]) for array in arrays], axis=0) for arrays in opposite]
    far_right, far_left = project(far, opposite, outs=2)
    from_left_late, from_right_late = shift(far_right, 1), shift(far_left, -1)
    (right_early,) = project(right, early, after(from_left, far_right), 0)
    (left_early,) = project(left, early, after(from_right, far_right), 3)
    right_in, left_in = shift(right_early, 1), shift(left_early, -1)
    (right_late,) = project(right, opposite, after(from_left_late, right_early, left_early), 0)
    (left_late,) = project(left, opposite, after(from_right_late, right_early, left_early), 1)
    right_late_in, left_late_in = shift(right_late, 1), shift(left_late, -1)
    own = mine_first(0, (after(own[0], left_late, right_late), own[1]))
    (own_early,) = project(own, early)
    (own_late,) = project(own, opposite)

    def summed(*terms):
        return sum(term[positions:].astype(jnp.float32) for term in terms).astype(jnp.bfloat16)

    early_terms = (own_early, right_in, left_in)
    late_terms = (own_late, right_late_in, left_late_in)
    return combine(
        valid_lengths,
        [*early_terms, swap(summed(*early_terms)), *late_terms, swap(summed(*late_terms))],
        [early_groups, late_groups],
        positions,
        width,
        side,
    )


def solution(mesh):
    in_specs = (
        P("dp", "sp", None),
        P("dp", "sp", None),
        P("dp", "sp", None),
        P("dp", "sp", None, None),
        P("dp", "sp", None, None),
        P("sp", "dp"),
        P(),
        P(),
    )
    out_specs = P("dp", "sp", None)
    return jax.shard_map(local, mesh=mesh, in_specs=in_specs, out_specs=out_specs, check_vma=False)
```

```python
import functools
import math

import jax
import jax.numpy as jnp
from jax import lax
from jax.experimental import pallas as pl
from jax.experimental.pallas import tpu as pltpu
from jax.sharding import PartitionSpec as P


NEGATIVE = -1e30
VMEM_LIMIT = 48 << 20
KEY_BLOCK = 4096
KEY_PIECE = 1024
ROW_CHUNK = 128


def trajectory(sibling):
    row = lax.axis_index("dp")
    return row + 1 - 2 * lax.rem(row, 2) if sibling else row


def attention_kernel(
    prefix_lengths,
    valid_lengths,
    q_ref,
    span_ref,
    k_ref,
    v_ref,
    o_ref,
    rows,
    high,
    total,
    *,
    distance,
    sibling,
    factor,
):
    step = pl.program_id(0)
    head_dim = k_ref.shape[1]
    positions = q_ref.shape[0]
    heads = o_ref.shape[1] // head_dim
    row_count = heads * positions
    key_block = k_ref.shape[0]
    chunk = min(ROW_CHUNK, row_count)
    parts = lax.axis_size("sp")
    me = lax.axis_index("sp")
    row = trajectory(sibling)
    length = prefix_lengths[row]

    def start_of(offset):
        return lax.rem(me + offset, parts) * positions

    first_position = start_of(distance)
    live = first_position < valid_lengths[row]

    def update(keys, values, usable):
        augmented = jnp.concatenate([values, jnp.ones_like(values)], axis=1)

        def score(start):
            return lax.dot_general(
                rows[pl.ds(start, chunk), :],
                keys,
                (((1,), (1,)), ((), ())),
                preferred_element_type=jnp.float32,
            )

        def fold(start, scores):
            if usable is not None:
                scores = jnp.where(usable(scores.shape), scores, NEGATIVE)
            block = pl.ds(start, chunk)
            before = high[block, :]
            after = jnp.maximum(before, jnp.max(scores, axis=1, keepdims=True))
            high[block, :] = after
            rescale = jnp.exp2((before - after) * factor)
            weights = jnp.exp2((scores - after[:, :1]) * factor).astype(jnp.bfloat16)
            total[block, :] = total[block, :] * jnp.concatenate([rescale, rescale], axis=1) + jnp.dot(
                weights, augmented, preferred_element_type=jnp.float32
            )

        following = score(0)
        for start in range(0, row_count, chunk):
            scores = following
            if start + chunk < row_count:
                following = score(start + chunk)
            fold(start, scores)

    @pl.when(jnp.logical_and(step == 0, live))
    def _():
        for head in range(heads):
            rows[head * positions : (head + 1) * positions, :] = q_ref[:, head * head_dim : (head + 1) * head_dim]
        high[...] = jnp.full_like(high, NEGATIVE)
        total[...] = jnp.zeros_like(total)

        def causal(shape):
            query = first_position + lax.rem(lax.broadcasted_iota(jnp.int32, shape, 0), positions)
            column = lax.broadcasted_iota(jnp.int32, shape, 1)
            key = start_of(0) + column
            for index in range(1, parts):
                key = jnp.where(column >= index * positions, start_of(index) + column - index * positions, key)
            return key <= query

        update(span_ref[:, :head_dim], span_ref[:, head_dim:], causal)

    before_block = (step - 1) * key_block

    @pl.when(jnp.logical_and(live, jnp.logical_and(step > 0, step * key_block <= length)))
    def _():
        update(k_ref[...], v_ref[...], None)

    @pl.when(
        jnp.logical_and(
            live,
            jnp.logical_and(step > 0, jnp.logical_and(before_block < length, step * key_block > length)),
        )
    )
    def _():
        piece = math.gcd(KEY_PIECE, key_block)

        @pl.loop(0, lax.div(length - before_block + piece - 1, piece))
        def _(index):
            begin = pl.multiple_of(index * piece, piece)

            def stored(shape):
                return before_block + begin + lax.broadcasted_iota(jnp.int32, shape, 1) < length

            update(k_ref[pl.ds(begin, piece), :], v_ref[pl.ds(begin, piece), :], stored)

    @pl.when(step == pl.num_programs(0) - 1)
    def _():
        @pl.when(live)
        def _():
            for head in range(heads):
                block = slice(head * positions, (head + 1) * positions)
                o_ref[:, head * head_dim : (head + 1) * head_dim] = (
                    total[block, :head_dim] / total[block, head_dim:]
                ).astype(o_ref.dtype)

        @pl.when(jnp.logical_not(live))
        def _():
            o_ref[...] = jnp.zeros_like(o_ref)


def attend(prefix_lengths, valid_lengths, query, fresh, distance, sibling, keys, values):
    positions, features = query.shape
    stored, head_dim = keys.shape
    key_block = math.gcd(KEY_BLOCK, stored)
    count = stored // key_block
    row_count = positions * features // head_dim

    def cached(step, prefix_lengths, valid_lengths):
        last = lax.div(prefix_lengths[trajectory(sibling)] - 1, key_block)
        return (jnp.clip(step - 1, 0, last), 0)

    def whole(step, *_):
        return (0, 0)

    flops = 8 * row_count * (stored + fresh.shape[0]) * head_dim
    return pl.pallas_call(
        functools.partial(
            attention_kernel, distance=distance, sibling=sibling, factor=math.log2(math.e) / math.sqrt(head_dim)
        ),
        grid_spec=pltpu.PrefetchScalarGridSpec(
            num_scalar_prefetch=2,
            grid=(count + 1,),
            in_specs=[pl.BlockSpec((positions, features), whole)]
            + [pl.BlockSpec(fresh.shape, whole)]
            + [pl.BlockSpec((key_block, head_dim), cached)] * 2,
            out_specs=pl.BlockSpec((positions, features), whole),
            scratch_shapes=[
                pltpu.VMEM((row_count, head_dim), jnp.bfloat16),
                pltpu.VMEM((row_count, head_dim), jnp.float32),
                pltpu.VMEM((row_count, 2 * head_dim), jnp.float32),
            ],
        ),
        out_shape=jax.ShapeDtypeStruct((positions, features), jnp.bfloat16),
        compiler_params=pltpu.CompilerParams(vmem_limit_bytes=VMEM_LIMIT),
        cost_estimate=pl.CostEstimate(
            flops=flops, bytes_accessed=4 * stored * head_dim, transcendentals=row_count * stored
        ),
        name="attend",
    )(prefix_lengths, valid_lengths, query, fresh, keys, values)


def project_kernel(*refs, adds, outs):
    count = len(adds)
    mine_ref, other_ref = refs[:2]
    w_refs = refs[2 : 2 + count]
    add_refs = refs[2 + count : -outs - 3]
    o_refs = refs[-outs - 3 : -3]
    both, held, arrivals = refs[-3:]
    copies = []
    for index in range(count):
        copy = pltpu.make_async_copy(w_refs[index], held.at[index], arrivals.at[index])
        copy.start()
        copies.append(copy)
    positions = mine_ref.shape[0]
    both[:positions, :] = mine_ref[...]
    both[positions:, :] = other_ref[...]
    pieces, width = held.shape[1], held.shape[3]
    share = count // outs
    for index, copy in enumerate(copies):
        copy.wait()
        o_ref = o_refs[index // share]
        for piece in range(0, pieces, 2):
            tile = jnp.concatenate([held[index, piece], held[index, piece + 1]], axis=1)
            product = jnp.dot(both[...], tile, preferred_element_type=jnp.float32)
            if adds[index] is not None:
                source, group = adds[index]
                begin = (group * pieces + piece) * width
                product = product + add_refs[source][:, begin : begin + 2 * width].astype(jnp.float32)
            begin = (index % share * pieces + piece) * width
            o_ref[:, begin : begin + 2 * width] = product.astype(o_ref.dtype)


def project(pair, weights, arrived=(), outs=1):
    positions, depth = pair[0].shape
    pieces, _, width = weights[0].shape
    rows = 2 * positions
    count = len(weights)
    columns = count * pieces * width
    adds = [
        (source, group) for source, array in enumerate(arrived) for group in range(array.shape[1] // (pieces * width))
    ]
    adds += [None] * (count - len(adds))
    whole = pl.BlockSpec(memory_space=pltpu.VMEM)
    return pl.pallas_call(
        functools.partial(project_kernel, adds=adds, outs=outs),
        in_specs=[whole] * 2 + [pl.BlockSpec(memory_space=pl.ANY)] * count + [whole] * len(arrived),
        out_specs=[whole] * outs,
        scratch_shapes=[
            pltpu.VMEM((rows, depth), jnp.bfloat16),
            pltpu.VMEM((count, pieces, depth, width), jnp.bfloat16),
            pltpu.SemaphoreType.DMA((count,)),
        ],
        out_shape=[jax.ShapeDtypeStruct((rows, columns // outs), jnp.bfloat16)] * outs,
        compiler_params=pltpu.CompilerParams(vmem_limit_bytes=VMEM_LIMIT),
        cost_estimate=pl.CostEstimate(
            flops=2 * rows * depth * columns, bytes_accessed=2 * depth * columns, transcendentals=0
        ),
        name="project",
    )(*pair, *weights, *arrived)


def place_of(row, side):
    chip = lax.div(row, 2)
    return lax.div(chip, side), lax.rem(chip, side)


def combine_kernel(valid_lengths, *refs, groups, width, side):
    o_ref = refs[-1]
    positions = o_ref.shape[1]
    start = lax.axis_index("sp") * positions
    row = lax.axis_index("dp")
    core = lax.rem(row, 2)
    y, z = place_of(row, side)
    keep = start + lax.broadcasted_iota(jnp.int32, (positions, width), 0) < valid_lengths[row]
    for part, members in enumerate(groups):
        own, first, second, arrived = refs[4 * part : 4 * part + 4]
        for index, (kind, offset) in enumerate(members):
            for step in range(side):
                dy, dz = (step, offset) if kind == 0 else (offset, step)
                piece = lax.rem(y + dy, side) * side + lax.rem(z + dz, side)
                columns = slice((index * side + step) * width, (index * side + step + 1) * width)
                total = (
                    own[:, columns].astype(jnp.float32)
                    + first[:, columns].astype(jnp.float32)
                    + second[:, columns].astype(jnp.float32)
                )
                for source, value in ((core, total.astype(o_ref.dtype)), (1 - core, arrived[:, columns])):
                    column = pl.multiple_of((2 * piece + source) * 2 * width + kind * width, width)
                    o_ref[0, :, pl.ds(column, width)] = jnp.where(keep, value, jnp.zeros_like(value))


def combine(valid_lengths, parts, groups, positions, width, side):
    columns = 4 * width * side * side
    return pl.pallas_call(
        functools.partial(combine_kernel, groups=groups, width=width, side=side),
        grid_spec=pltpu.PrefetchScalarGridSpec(
            num_scalar_prefetch=1,
            grid=(1,),
            in_specs=[pl.BlockSpec((positions, part.shape[1]), lambda step, _: (0, 0)) for part in parts],
            out_specs=pl.BlockSpec((1, positions, columns), lambda step, _: (0, 0, 0)),
        ),
        out_shape=jax.ShapeDtypeStruct((1, positions, columns), jnp.bfloat16),
        compiler_params=pltpu.CompilerParams(vmem_limit_bytes=VMEM_LIMIT),
        name="combine",
    )(valid_lengths, *parts)


def local(
    queries,
    rotated_span_keys,
    span_value_heads,
    cache_keys,
    cached_prefix_values,
    out_weight,
    prefix_lengths,
    valid_lengths,
):
    parts = lax.axis_size("sp")
    rows = lax.axis_size("dp")
    me = lax.axis_index("sp")
    positions = queries.shape[1]
    head_dim = cache_keys.shape[3]
    features = queries.shape[2] // parts

    side = math.isqrt(rows // 2)
    width = out_weight.shape[1] // 2

    def shift(array, distance):
        return lax.ppermute(array, "sp", [(i, (i + distance) % parts) for i in range(parts)])

    def swap(array):
        return lax.ppermute(array, "dp", [(i, i ^ 1) for i in range(rows)])

    def across(array, dy, dz):
        pairs = []
        for i in range(rows):
            y, z, core = i // (2 * side), (i // 2) % side, i % 2
            pairs.append((i, (((y + dy) % side) * side + (z + dz) % side) * 2 + core))
        return lax.ppermute(array, "dp", pairs)

    def after(value, *others):
        return lax.optimization_barrier((value, *others))[0]

    def part_of(array, owner, size):
        return lax.dynamic_slice_in_dim(array, owner * size, size, 1)

    def gather_line(piece, dy, dz):
        return [piece, across(piece, -dy, -dz), across(piece, 2 * dy, 2 * dz), across(piece, dy, dz)]

    pieces = [out_weight[:, :width], out_weight[:, width:]]
    lines = [gather_line(pieces[0], 1, 0), gather_line(pieces[1], 0, 1)]

    def shift_across(array, distance):
        pairs = [
            (row * parts + i, (row ^ 1) * parts + (i + distance) % parts) for row in range(rows) for i in range(parts)
        ]
        return lax.ppermute(array, ("dp", "sp"), pairs)

    fresh, query = [None] * parts, [None] * parts
    for distance in (2, 1, 3, 0):
        owner = lax.rem(me + distance, parts)
        pair = jnp.concatenate(
            [part_of(rotated_span_keys[0], owner, head_dim), part_of(span_value_heads[0], owner, head_dim)], axis=1
        )
        fresh[(parts - distance) % parts] = shift(pair, distance) if distance else pair
    for distance in (3, 2, 1, 0):
        part = part_of(queries[0], lax.rem(me + distance, parts), features)
        if distance == 0:
            query[0] = swap(part)
        elif distance == 2:
            query[2] = shift_across(part, distance)
        else:
            query[parts - distance] = shift(part, distance)
    fresh = jnp.concatenate(fresh, axis=0)
    keys, values = cache_keys[0, 0], cached_prefix_values[0, 0]
    stores = {False: (fresh, keys, values), True: (swap(fresh), swap(keys), swap(values))}

    def attended(distance, *waits):
        sibling = distance % 2 == 0
        fresh, keys, values = stores[sibling]
        result = attend(
            prefix_lengths,
            valid_lengths,
            after(query[distance], *waits),
            fresh,
            distance,
            sibling,
            keys,
            values,
        )
        return result, swap(result)

    def mine_first(distance, pair):
        return pair[::-1] if distance % 2 == 0 else pair

    lines = [jnp.stack(line) for line in lines]
    behind = [across(lines[0], 0, 1), across(lines[1], 1, 0)]
    ahead = [across(lines[0], 0, -1), across(lines[1], -1, 0)]

    right = attended(1, *lines)
    far = attended(2, right[0])
    half = side // 2
    early = [[lines[kind], ahead[kind], behind[kind]] for kind in range(2)]

    first_behind, first_ahead = after(behind[0][:half], far[0]), after(ahead[0][half:], far[0])
    opposite = [[across(first_behind, 0, 1), across(first_ahead, 0, -1)]]
    far = mine_first(2, (after(far[0], first_behind, first_ahead), far[1]))
    far_right, far_left = project(far, early[0] + early[1], outs=2)
    from_left, from_right = shift(far_right, 1), shift(far_left, -1)
    second_behind, second_ahead = after(behind[1][:half], far_right), after(ahead[1][half:], far_right)
    opposite.append([across(second_behind, 1, 0), across(second_ahead, -1, 0)])
    left = attended(3, far_right, second_behind, second_ahead)
    own = attended(0, left[0])
    opposite = [jnp.concatenate([after(array, own[0]) for array in arrays], axis=0) for arrays in opposite]
    far_right, far_left = project(far, opposite, outs=2)
    from_left_late, from_right_late = shift(far_right, 1), shift(far_left, -1)
    groups = [early[kind] + [opposite[kind]] for kind in range(2)]
    (right_free,) = project((after(right[0], far_right), right[1]), groups[1])
    (left_free,) = project((after(left[0], far_right), left[1]), groups[0])
    right_in = [None, shift(right_free, 1)]
    left_in = [shift(left_free, -1), None]
    (right_sum,) = project(right, groups[0], (after(from_left, right_free, left_free), from_left_late))
    (left_sum,) = project(left, groups[1], (after(from_right, right_free, left_free), from_right_late))
    right_in[0] = shift(right_sum, 1)
    left_in[1] = shift(left_sum, -1)
    own = mine_first(0, (after(own[0], left_sum, right_sum), own[1]))
    own_in = [project(own, groups[kind])[0] for kind in range(2)]

    def summed(*terms):
        return sum(term[positions:].astype(jnp.float32) for term in terms).astype(jnp.bfloat16)

    terms = []
    for kind in range(2):
        mine = (own_in[kind], right_in[kind], left_in[kind])
        terms += [*mine, swap(summed(*mine))]
    members = [[(kind, offset) for offset in (0, 1, 3, 2)] for kind in range(2)]
    return combine(valid_lengths, terms, members, positions, width, side)


def solution(mesh):
    in_specs = (
        P("dp", "sp", None),
        P("dp", "sp", None),
        P("dp", "sp", None),
        P("dp", "sp", None, None),
        P("dp", "sp", None, None),
        P("sp", "dp"),
        P(),
        P(),
    )
    out_specs = P("dp", "sp", None)
    return jax.shard_map(local, mesh=mesh, in_specs=in_specs, out_specs=out_specs, check_vma=False)
```
